32 devices in a mesh: seq: 8 (over z, y), head: 4 (over x, core).
Axes of the slice: x: 2, y: 2, z: 4, core: 2. Of those that a mesh axis runs over, the one named last changes fastest.
Arguments:
- tokens: bfloat16 [2048, 2560], P('seq'), may hold values from -6 to 6
- x_weight: bfloat16 [2560, 5120], P(None, 'head'), may hold values from -0.125 to 0.125
- b_input: bfloat16 [2048, 128], P('seq'), may hold values from -6 to 6
- c_input: bfloat16 [2048, 128], P('seq'), may hold values from -0.52734375 to 0.52734375
- log_decay: float32 [2048, 80], P('seq', 'head'), may hold values from -1 to 0
- step_size: float32 [2048, 80], P('seq', 'head'), may hold values from 0 to 1
- cotangent: bfloat16 [2048, 5120], P('seq', 'head'), may hold values from -6 to 6
Outputs:
- ssd_out: bfloat16 [2048, 5120], P('seq', 'head')
- tokens_grad: bfloat16 [2048, 2560], P('seq', 'head')
- weight_grad: float32 [2560, 5120], P('seq', 'head')
- decay_grad: float32 [2048, 80], P('seq', 'head')
The draws below stay inside these ranges and needn't reach their ends.
All inputs are finite; a program needn't handle non-finite values.
Results may differ from the reference program's by a relative error of at most 0.0061.
Values sent between devices are 32-bit elements; how exact they have to be, the bound alone decides.
A program may use at most 192 MiB of HBM per device.

```python
import jax
import jax.numpy as jnp
from jax import lax

D = 2560
HEAD_TOTAL = 80
HDIM = 64
NSTATE = 128
SPAN = 256
TOK_DEV = 256
TOKEN_POSITIONS = 2048


def head_rates(key):
    base_key = jax.random.fold_in(key, 7)
    key_list = jax.random.split(base_key, 6)
    fast_share = 4
    fast_heads = jax.random.randint(key_list[0], (HEAD_TOTAL,), 0, 8) < fast_share
    fast_base = jax.random.uniform(key_list[1], (HEAD_TOTAL,), jnp.float32, 1.0 / 50.0, 1.0 / 30.0)
    slow_base = jnp.full((HEAD_TOTAL,), 0.5 / TOKEN_POSITIONS, jnp.float32)
    base_rate = jnp.where(fast_heads, fast_base, slow_base)
    block_factor = jnp.exp(jax.random.uniform(key_list[2], (TOKEN_POSITIONS // TOK_DEV, HEAD_TOTAL), jnp.float32, -0.69, 0.69))
    block_factor = jnp.repeat(block_factor, TOK_DEV, axis=0)
    return (base_rate[None, :] * block_factor, key_list)


def draw_log_decay(key, part):
    decay_rates, key_list = head_rates(key)
    coarse_estimate = jax.random.uniform(key_list[3], (TOKEN_POSITIONS, HEAD_TOTAL), jnp.float32, 0.6, 1.4)
    sample_locations = jax.random.randint(key_list[4], (3, HEAD_TOTAL), 0, TOKEN_POSITIONS)
    loss_values = jax.random.uniform(key_list[5], (3, HEAD_TOTAL), jnp.float32, 0.2, 0.4)
    token_positions = lax.broadcasted_iota(jnp.int32, (TOKEN_POSITIONS, HEAD_TOTAL), 0)
    segment_groups = jnp.zeros((TOKEN_POSITIONS, HEAD_TOTAL), jnp.float32)
    for segment_index in range(3):
        segment_groups = segment_groups + jnp.where(token_positions == sample_locations[segment_index][None, :], -jnp.log(1.0 - loss_values[segment_index])[None, :], 0.0)
    return -(decay_rates * coarse_estimate + segment_groups)


def draw_step_size(key, part):
    decay_rates, key_list = head_rates(key)
    spread = jax.random.uniform(jax.random.fold_in(key, 19), (TOKEN_POSITIONS, HEAD_TOTAL), jnp.float32, 0.7, 1.3)
    return jnp.sqrt(2.0 * decay_rates) * spread


def spiked(entries, rng, source, target, shards_of, factor):
    owner, partner = [(jnp.arange(entries.shape[dim]) // (entries.shape[dim] // shards_of)).reshape([-1 if axis == dim else 1 for axis in range(entries.ndim)]) for dim in (source, target)]
    chosen = jax.random.permutation(rng, shards_of)[partner]
    strong = (owner == chosen) | (owner == (partner + shards_of // 2) % shards_of)
    return jnp.where(strong, factor * entries, entries)


def block_levels(rng, dims, shards, smallest, high):
    gain, own = 1.0, jax.random.fold_in(rng, 6)
    for dim, parts in shards:
        steps = jnp.exp(jax.random.uniform(jax.random.fold_in(own, dim), (parts,), jnp.float32, smallest / len(shards), high / len(shards)))
        gain = gain * jnp.repeat(steps, dims[dim] // parts).reshape([-1 if axis == dim else 1 for axis in range(len(dims))])
    return gain


def normal_values(key, dims, scale, most, shards=(), kind=jnp.bfloat16):
    values = jax.random.normal(key, dims, jnp.float32) * scale
    if len(shards) > 0:
        values = block_levels(key, dims, shards, -0.22, 0.18) * values
    return jnp.clip(values, min=-most, max=most).astype(kind)


def gaussian_with(rng, dims, scale, limit, shards, heavy, kind=jnp.bfloat16):
    result = scale * jax.random.normal(rng, dims, jnp.float32)
    if shards:
        result = result * block_levels(rng, dims, shards, -0.22, 0.18)
    return jnp.clip(spiked(result, jax.random.fold_in(rng, 3), *heavy), -limit, limit).astype(kind)


def setup_inputs(seed: int = 0) -> dict:
    keys = jax.random.split(jax.random.key(seed), 8)
    return {
        "tokens": gaussian_with(keys[0], (TOKEN_POSITIONS, D), 1.0, 6.0, ((0, 8),), (0, 1, 8, 2.0)),
        "x_weight": normal_values(keys[1], (D, HEAD_TOTAL * HDIM), D ** -0.5, 0.125, ((1, 4),)),
        "b_input": normal_values(keys[2], (TOKEN_POSITIONS, NSTATE), 1.0, 6.0, ((0, 8),)),
        "c_input": normal_values(keys[3], (TOKEN_POSITIONS, NSTATE), (NSTATE ** -0.5), 0.52734375, ((0, 8),)),
        "log_decay": draw_log_decay(jax.random.fold_in(keys[7], 71), 0),
        "step_size": draw_step_size(jax.random.fold_in(keys[7], 71), 0),
        "cotangent": normal_values(keys[6], (TOKEN_POSITIONS, HEAD_TOTAL * HDIM), 1.0, 6.0, ((0, 8), (1, 4))),
    }


highest = lax.Precision.HIGHEST


def span_tables(length):
    row_ids = lax.broadcasted_iota(jnp.int32, (length, length), 0)
    col_ids = lax.broadcasted_iota(jnp.int32, (length, length), 1)
    return row_ids >= col_ids, row_ids > col_ids


def span_mixing(b_span, c_span, cum_span, lower_mask):
    scores = jnp.dot(c_span, b_span.T, preferred_element_type=jnp.float32)
    cum_heads = cum_span.T
    log_gap = cum_heads[:, :, None] - cum_heads[:, None, :]
    return scores[None] * jnp.exp(jnp.where(lower_mask[None], log_gap, -jnp.inf))


def span_weights(b_span, c_span, cum_span):
    span_end = cum_span[-1]
    b_weighted = (jnp.exp(span_end[None, :] - cum_span)[:, :, None] * b_span.astype(jnp.float32)[:, None, :]).astype(jnp.bfloat16)
    c_weighted = (jnp.exp(cum_span)[:, :, None] * c_span.astype(jnp.float32)[:, None, :]).astype(jnp.bfloat16)
    return b_weighted, c_weighted, jnp.exp(span_end)


def reference(tokens, x_weight, b_input, c_input, log_decay, step_size, cotangent):
    token_count = tokens.shape[0]
    span_count = token_count // SPAN
    pre_act = jnp.dot(tokens, x_weight, preferred_element_type=jnp.float32)
    activated = jax.nn.silu(pre_act)
    x_scaled = (activated.reshape(token_count, HEAD_TOTAL, HDIM) * step_size[:, :, None]).astype(jnp.bfloat16)
    lower_mask, strict_mask = span_tables(SPAN)
    lower_ones = lower_mask.astype(jnp.float32)
    strict_ones = strict_mask.astype(jnp.float32)
    cum_log = jnp.einsum('qr,krh->kqh', lower_ones, log_decay.reshape(span_count, SPAN, HEAD_TOTAL), precision=highest)
    x_spans = x_scaled.reshape(span_count, SPAN, HEAD_TOTAL, HDIM)
    grad_spans = cotangent.reshape(span_count, SPAN, HEAD_TOTAL, HDIM)
    b_spans = b_input.reshape(span_count, SPAN, NSTATE)
    c_spans = c_input.reshape(span_count, SPAN, NSTATE)
    zero_state = jnp.zeros((HEAD_TOTAL, NSTATE, HDIM), jnp.float32)

    def forward_step(carry_state, pieces):
        x_span, b_span, c_span, cum_span = pieces
        b_weighted, c_weighted, span_factor = span_weights(b_span, c_span, cum_span)
        local_state = jnp.einsum('qhn,qhp->hnp', b_weighted.astype(jnp.float32), x_span.astype(jnp.float32))
        return span_factor[:, None, None] * carry_state + local_state, carry_state

    last_state, prior_states = lax.scan(forward_step, zero_state, (x_spans, b_spans, c_spans, cum_log))

    def backward_step(carry_state, pieces):
        grad_span, b_span, c_span, cum_span = pieces
        b_weighted, c_weighted, span_factor = span_weights(b_span, c_span, cum_span)
        gathered = jnp.einsum('qhn,qhp->hnp', c_weighted.astype(jnp.float32), grad_span.astype(jnp.float32))
        return gathered + span_factor[:, None, None] * carry_state, carry_state

    first_adjoint, later_adjoints = lax.scan(backward_step, zero_state, (grad_spans, b_spans, c_spans, cum_log), reverse=True)

    def span_main(pieces):
        x_span, grad_span, b_span, c_span, cum_span, prior_state, adjoint = pieces
        mixing = span_mixing(b_span, c_span, cum_span, lower_mask)
        rounded = mixing.astype(jnp.bfloat16).astype(jnp.float32)
        b_weighted, c_weighted, span_factor = span_weights(b_span, c_span, cum_span)
        x_float = x_span.astype(jnp.float32)
        grad_float = grad_span.astype(jnp.float32)
        inner_part = jnp.einsum('hqr,rhp->qhp', rounded, x_float)
        carried = jnp.einsum('qhn,hnp->qhp', c_weighted.astype(jnp.float32), prior_state, precision=highest)
        output = (inner_part + carried).astype(jnp.bfloat16)
        back_inner = jnp.einsum('hqr,qhp->rhp', rounded, grad_float)
        back_carried = jnp.einsum('rhn,hnp->rhp', b_weighted.astype(jnp.float32), adjoint, precision=highest)
        grad_x = back_inner + back_carried
        products = jnp.einsum('qhp,rhp->hqr', grad_float, x_float)
        pair_terms = jnp.where(strict_mask[None], mixing * products, 0.0)
        shifts = jnp.sum(pair_terms, axis=2) - jnp.sum(pair_terms, axis=1)
        arrival = jnp.sum(grad_float * carried, axis=2)
        departure = jnp.sum(x_float * back_carried, axis=2)
        through = span_factor * jnp.sum(prior_state * adjoint, axis=(1, 2))
        decay_part = jnp.dot(lower_ones.T, shifts.T + arrival, precision=highest)
        decay_part = decay_part + jnp.dot(strict_ones, departure, precision=highest) + through[None, :]
        return output, grad_x, decay_part

    outputs, grad_x, decay_grad = lax.map(span_main, (x_spans, grad_spans, b_spans, c_spans, cum_log, prior_states, later_adjoints))
    sigmoid_pre = jax.nn.sigmoid(pre_act)
    scaled_grad = (grad_x.reshape(token_count, HEAD_TOTAL, HDIM) * step_size[:, :, None]).reshape(token_count, HEAD_TOTAL * HDIM)
    pre_grad = (scaled_grad * sigmoid_pre * (1.0 + pre_act * (1.0 - sigmoid_pre))).astype(jnp.bfloat16)
    weight_grad = lax.dot_general(tokens, pre_grad, (((0,), (0,)), ((), ())), preferred_element_type=jnp.float32)
    tokens_grad = lax.dot_general(pre_grad, x_weight, (((1,), (1,)), ((), ())), preferred_element_type=jnp.float32).astype(jnp.bfloat16)
    ssd_out = outputs.reshape(token_count, HEAD_TOTAL * HDIM)
    return ssd_out, tokens_grad, weight_grad, decay_grad.reshape(token_count, HEAD_TOTAL)
```

```python
import functools
import math

import jax
import jax.numpy as jnp
from jax import lax
from jax.experimental import pallas as pl
from jax.experimental.pallas import tpu as pltpu
from jax.sharding import PartitionSpec as P

SPAN = 256
LANES = 128
MESH = pl.DeviceIdType.MESH
highest = lax.Precision.HIGHEST
f32 = jnp.float32
bf16 = jnp.bfloat16


def dot_f32(a, b, dims=(((1,), (0,)), ((), ()))):
    return lax.dot_general(a, b, dims, preferred_element_type=f32)


def dot_exact(a, b, dims=(((1,), (0,)), ((), ()))):
    return lax.dot_general(a, b, dims, preferred_element_type=f32, precision=highest)


ROWS = (((0,), (0,)), ((), ()))
COLS = (((1,), (1,)), ((), ()))


def split_two(a):
    high = a.astype(bf16)
    return high, (a - high.astype(f32)).astype(bf16)


def span_kernel(n, *refs):
    tok, xw_hbm, b_ref, c_ref, ld, st, cot, y_ref, pg_ref, dg_ref = refs[:10]
    (x_s, pre_s, ce_s, st_s, cum_t, inner_s, back_s, score_s, loc_f, loc_b, out_f, out_b,
     prior, adj, q1_s, q2_s, th_s, xw, xw_sem, send_f, recv_f, send_b, recv_b) = refs[10:]
    d = lax.axis_index("seq")
    rows, width = cot.shape
    heads = ld.shape[0]
    hdim = width // heads
    pairs = width // LANES
    per = LANES // hdim
    load = pltpu.make_async_copy(xw_hbm, xw, xw_sem)
    load.start()

    barrier = pltpu.get_barrier_semaphore()
    for o in (1, n - 1):
        pl.semaphore_signal(barrier, 1, device_id={"seq": lax.rem(d + o, n)}, device_id_type=MESH)
    pl.semaphore_wait(barrier, 2)

    row_ids = lax.broadcasted_iota(jnp.int32, (rows, rows), 0)
    col_ids = lax.broadcasted_iota(jnp.int32, (rows, rows), 1)
    lower = row_ids >= col_ids
    lower_ones = lower.astype(f32)
    decay = ld[...]
    cum = dot_exact(lower_ones, decay, COLS)
    cum_t[...] = dot_exact(decay, lower_ones, COLS)
    spread = (lax.broadcasted_iota(jnp.int32, (heads, width), 0)
              == lax.broadcasted_iota(jnp.int32, (heads, width), 1) // hdim).astype(f32)
    wide_cum = dot_exact(cum, spread)
    wide_step = dot_exact(st[...], spread, ROWS)
    for p in range(pairs):
        ce_s[p] = wide_cum[:, p * LANES:(p + 1) * LANES]
        st_s[p] = wide_step[:, p * LANES:(p + 1) * LANES]
    b_val, c_val = b_ref[...], c_ref[...]
    score_s[...] = jnp.where(lower, dot_f32(c_val, b_val, COLS), 0.0)
    q1_s[...] = jnp.zeros_like(q1_s)
    q2_s[...] = jnp.zeros_like(q2_s)
    th_s[...] = jnp.zeros_like(th_s)

    load.wait()
    step_cols = 2 * LANES
    for k in range(width // step_cols):
        cols = slice(k * step_cols, (k + 1) * step_cols)
        ce = wide_cum[:, cols]
        gw = (cot[:, cols].astype(f32) * jnp.exp(ce)).astype(bf16)
        grad_k = dot_f32(c_val, gw, ROWS)
        pre = dot_f32(tok[...], xw[:, cols])
        act = pre / (1.0 + jnp.exp(-pre))
        xk = (act * wide_step[:, cols]).astype(bf16)
        xwk = (xk.astype(f32) * jnp.exp(ce[rows - 1:rows] - ce)).astype(bf16)
        state_k = dot_f32(b_val, xwk, ROWS)
        for i in range(2):
            at = slice(i * LANES, (i + 1) * LANES)
            pre_s[2 * k + i] = pre[:, at]
            x_s[2 * k + i] = xk[:, at]
            loc_b[2 * k + i] = grad_k[:, at]
            loc_f[2 * k + i] = state_k[:, at]

    @pl.when(d == 0)
    def _():
        prior[...] = jnp.zeros_like(prior)

    @pl.when(d == n - 1)
    def _():
        adj[...] = jnp.zeros_like(adj)

    def fcopy(k):
        return pltpu.make_async_remote_copy(
            src_ref=out_f.at[k], dst_ref=prior.at[k], send_sem=send_f.at[k], recv_sem=recv_f.at[k],
            device_id={"seq": lax.rem(d + 1, n)}, device_id_type=MESH)

    def bcopy(k):
        return pltpu.make_async_remote_copy(
            src_ref=out_b.at[k], dst_ref=adj.at[k], send_sem=send_b.at[k], recv_sem=recv_b.at[k],
            device_id={"seq": lax.rem(d + n - 1, n)}, device_id_type=MESH)

    lane = lax.broadcasted_iota(jnp.int32, (rows, LANES), 1)

    def mix(p):
        ce = ce_s[p]
        xp = x_s[p]
        gp = cot[:, pl.ds(pl.multiple_of(p * LANES, LANES), LANES)]
        inner = back = None
        for i in range(per):
            gap = ce[:, i * hdim:i * hdim + 1] - cum_t[pl.ds(per * p + i, 1), :]
            m = (score_s[...] * jnp.exp(jnp.minimum(gap, 0.0))).astype(bf16)
            inner_i = dot_f32(m, xp)
            back_i = dot_f32(m, gp, ROWS)
            if inner is None:
                inner, back = inner_i, back_i
            else:
                inner = jnp.where(lane < i * hdim, inner, inner_i)
                back = jnp.where(lane < i * hdim, back, back_i)
        inner_s[p] = inner
        back_s[p] = back

    def finish(p):
        ce = ce_s[p]
        end = ce[rows - 1:rows]
        at = pl.ds(pl.multiple_of(p * LANES, LANES), LANES)
        pr, ad = prior[p], adj[p]
        hi, lo = split_two(ad)
        bc = jnp.exp(end - ce) * (dot_f32(b_val, hi) + dot_f32(b_val, lo))
        bi = back_s[p]
        pre = pre_s[p]
        sig = 1.0 / (1.0 + jnp.exp(-pre))
        pg = (bi + bc) * st_s[p] * sig * (1.0 + pre * (1.0 - sig))
        pg_ref[:, at] = pg.astype(bf16).astype(f32)
        grad = cot[:, at].astype(f32)
        x = x_s[p].astype(f32)
        hi, lo = split_two(pr)
        y = inner_s[p] + jnp.exp(ce) * (dot_f32(c_val, hi) + dot_f32(c_val, lo))
        y_ref[:, at] = y.astype(bf16)
        pick = (lax.broadcasted_iota(jnp.int32, (LANES, heads), 0) // hdim + per * p
                == lax.broadcasted_iota(jnp.int32, (LANES, heads), 1)).astype(f32)
        q1_s[...] += dot_exact(grad * y - x * bi, pick)
        q2_s[...] += dot_exact(x * bc, pick)
        through = jnp.exp(end) * jnp.sum(pr * ad, axis=0, keepdims=True)
        th_s[...] += dot_exact(pick, jnp.broadcast_to(through, (8, LANES)), (((0,), (1,)), ((), ())))

    def chain(s, carry):
        kf = s - d

        @pl.when(jnp.logical_and(kf >= 0, kf < pairs))
        def _():
            @pl.when(d > 0)
            def _():
                fcopy(kf).wait_recv()

            @pl.when(d < n - 1)
            def _():
                out_f[kf] = jnp.exp(ce_s[kf, rows - 1:rows, :]) * prior[kf] + loc_f[kf]
                fcopy(kf).start()

        kb = s - (n - 1 - d)

        @pl.when(jnp.logical_and(kb >= 0, kb < pairs))
        def _():
            @pl.when(d < n - 1)
            def _():
                bcopy(kb).wait_recv()

            @pl.when(d > 0)
            def _():
                out_b[kb] = jnp.exp(ce_s[kb, rows - 1:rows, :]) * adj[kb] + loc_b[kb]
                bcopy(kb).start()

        @pl.when(s < pairs)
        def _():
            mix(s)

        ks = s - (n - 1)

        @pl.when(jnp.logical_and(ks >= 0, ks < pairs))
        def _():
            finish(ks)

        return carry

    lax.fori_loop(0, n - 1 + pairs, chain, 0)

    strict_ones = (row_ids > col_ids).astype(f32)
    dg_ref[...] = (dot_exact(q1_s[...], lower_ones, ROWS)
                   + dot_exact(q2_s[...], strict_ones, (((0,), (1,)), ((), ()))) + th_s[:, 0:1])

    @pl.when(d < n - 1)
    def _():
        def one(k, carry):
            fcopy(k).wait_send()
            return carry
        lax.fori_loop(0, pairs, one, 0)

    @pl.when(d > 0)
    def _():
        def one(k, carry):
            bcopy(k).wait_send()
            return carry
        lax.fori_loop(0, pairs, one, 0)


def span_call(n, *args):
    _, x_weight, b_input, _, log_decay, _, cotangent = args
    depth = x_weight.shape[0]
    rows, width = cotangent.shape
    heads, state = log_decay.shape[0], b_input.shape[1]
    pairs = width // LANES
    vm = pl.BlockSpec(memory_space=pltpu.VMEM)
    wide = pltpu.VMEM((pairs, rows, LANES), f32)
    states = pltpu.VMEM((pairs, state, LANES), f32)
    dma = pltpu.SemaphoreType.DMA
    scratch = [
        pltpu.VMEM((pairs, rows, LANES), bf16), wide, wide, wide, pltpu.VMEM((heads, rows), f32),
        wide, wide, pltpu.VMEM((rows, rows), f32), states, states, states, states, states, states,
        pltpu.VMEM((rows, heads), f32), pltpu.VMEM((rows, heads), f32), pltpu.VMEM((heads, 8), f32),
        pltpu.VMEM(x_weight.shape, bf16), dma(()), dma((pairs,)), dma((pairs,)), dma((pairs,)), dma((pairs,))]
    outs = [jax.ShapeDtypeStruct((rows, width), bf16), jax.ShapeDtypeStruct((rows, width), f32),
            jax.ShapeDtypeStruct((heads, rows), f32)]
    return pl.pallas_call(
        functools.partial(span_kernel, n),
        out_shape=outs,
        in_specs=[vm, pl.BlockSpec(memory_space=pl.ANY)] + [vm] * (len(args) - 2),
        out_specs=[vm] * len(outs),
        scratch_shapes=scratch,
        compiler_params=pltpu.CompilerParams(
            collective_id=0, has_side_effects=True, vmem_limit_bytes=60 << 20),
        cost_estimate=pl.CostEstimate(
            flops=6 * rows * depth * width, bytes_accessed=12 << 20, transcendentals=1 << 20),
        name="span",
    )(*args)


def hub_kernel(n, nh, *refs):
    tok, xw_hbm, b_ref, c_ref, ld, st, cot, y_ref, dg_ref, wg_ref, tg_ref = refs[:11]
    (x_s, pre_s, ce_s, st_s, cum_t, inner_s, back_s, bc_s, score_s, loc_f, loc_b, out_f, out_b, prior, adj,
     q1_s, q2_s, th_s, xw, pg_s, pg_t, gat, tsend, tk, tok_t, w_own, w_oth, w_alpha, w_beta, y_got, o_got,
     part, got, xw_sem, send_f, recv_f, send_b, recv_b, pg_send, pg_recv, rl_send, t_send, tk_recv, tf_send,
     tx_send, y_send, y_recv, a_send, a_recv, b_send, b_recv, o_send, o_recv, g_send, g_recv) = refs[11:]
    d, h = lax.axis_index("seq"), lax.axis_index("head")
    rows, width = cot.shape
    depth = tok.shape[1]
    heads = ld.shape[0]
    hdim = width // heads
    pairs = width // LANES
    per = LANES // hdim
    quarter, half = rows // nh, depth // 2
    unit = depth // (2 * n)
    z, y = d // 2, lax.rem(d, 2)
    side = z // 2
    hub = jnp.logical_or(z == 1, z == 2)
    rim = jnp.logical_not(hub)
    d_near = (1 + side) * 2 + y
    d_far = (2 - side) * 2 + y
    d_rim = 3 * side * 2 + y
    d_y = d + 1 - 2 * y
    hx = lax.rem(h + 2, nh)
    hc = h + 1 - 2 * lax.rem(h, 2)
    hxc = lax.rem(hc + 2, nh)
    load = pltpu.make_async_copy(xw_hbm, xw, xw_sem)
    load.start()

    def remote(src, dst, send, recv, **to):
        return pltpu.make_async_remote_copy(
            src_ref=src, dst_ref=dst, send_sem=send, recv_sem=recv, device_id=to, device_id_type=MESH)

    barrier = pltpu.get_barrier_semaphore()
    for o in range(1, n):
        pl.semaphore_signal(barrier, 1, device_id={"seq": lax.rem(d + o, n)}, device_id_type=MESH)
    for o in range(1, nh):
        pl.semaphore_signal(barrier, 1, device_id={"head": lax.rem(h + o, nh)}, device_id_type=MESH)

    def token_rows(q, which):
        return tok[pl.ds(pl.multiple_of(q * quarter, quarter), quarter),
                   pl.ds(pl.multiple_of(which * half, half), half)].astype(f32)

    def t_far():
        slot = jnp.where(rim, 2, 1)
        return remote(tsend.at[2], tk.at[slot, h], t_send.at[2], tk_recv.at[slot, h], seq=d_far)

    def t_near(i, q):
        return remote(tsend.at[i], tk.at[0, q], t_send.at[i], tk_recv.at[0, q], seq=d_near)

    tsend[2] = token_rows(h, 1 - side)

    @pl.when(rim)
    def _():
        tsend[0] = token_rows(h, side)
        tsend[1] = token_rows(hx, side)

    row_ids = lax.broadcasted_iota(jnp.int32, (rows, rows), 0)
    col_ids = lax.broadcasted_iota(jnp.int32, (rows, rows), 1)
    lower = row_ids >= col_ids
    lower_ones = lower.astype(f32)
    decay = ld[...]
    cum = dot_exact(lower_ones, decay, COLS)
    spread = (lax.broadcasted_iota(jnp.int32, (heads, width), 0)
              == lax.broadcasted_iota(jnp.int32, (heads, width), 1) // hdim).astype(f32)
    wide_cum = dot_exact(cum, spread)
    step_cols = 2 * LANES
    for k in range(width // step_cols):
        cols = slice(k * step_cols, (k + 1) * step_cols)
        ce = wide_cum[:, cols]
        gw = (cot[:, cols].astype(f32) * jnp.exp(ce)).astype(bf16)
        grad_k = dot_f32(c_ref[...], gw, ROWS)
        for i in range(2):
            at = slice(i * LANES, (i + 1) * LANES)
            ce_s[2 * k + i] = ce[:, at]
            loc_b[2 * k + i] = grad_k[:, at]

    @pl.when(d == 0)
    def _():
        prior[...] = jnp.zeros_like(prior)

    @pl.when(d == n - 1)
    def _():
        adj[...] = jnp.zeros_like(adj)

    pl.semaphore_wait(barrier, n + nh - 2)
    t_far().start()

    @pl.when(rim)
    def _():
        t_near(0, h).start()
        t_near(1, hx).start()

    def fcopy(k):
        return remote(out_f.at[k], prior.at[k], send_f.at[k], recv_f.at[k], seq=lax.rem(d + 1, n))

    def bcopy(k):
        return remote(out_b.at[k], adj.at[k], send_b.at[k], recv_b.at[k], seq=lax.rem(d + n - 1, n))

    def forward(k):
        @pl.when(d > 0)
        def _():
            fcopy(k).wait_recv()

        @pl.when(d < n - 1)
        def _():
            out_f[k] = jnp.exp(ce_s[k, rows - 1:rows, :]) * prior[k] + loc_f[k]
            fcopy(k).start()

    def backward(k):
        @pl.when(d < n - 1)
        def _():
            bcopy(k).wait_recv()

        @pl.when(d > 0)
        def _():
            out_b[k] = jnp.exp(ce_s[k, rows - 1:rows, :]) * adj[k] + loc_b[k]
            bcopy(k).start()

    def prepare():
        cum_t[...] = dot_exact(decay, lower_ones, COLS)
        wide_step = dot_exact(st[...], spread, ROWS)
        for p in range(pairs):
            st_s[p] = wide_step[:, p * LANES:(p + 1) * LANES]
        score_s[...] = jnp.where(lower, dot_f32(c_ref[...], b_ref[...], COLS), 0.0)
        q1_s[...] = jnp.zeros_like(q1_s)
        q2_s[...] = jnp.zeros_like(q2_s)
        th_s[...] = jnp.zeros_like(th_s)
        load.wait()

    def project(k):
        pre = dot_f32(tok[...], xw[:, pl.ds(pl.multiple_of(k * step_cols, step_cols), step_cols)])
        for i in range(2):
            p = 2 * k + i
            pre_i = pre[:, i * LANES:(i + 1) * LANES]
            ce = ce_s[p]
            act = pre_i / (1.0 + jnp.exp(-pre_i))
            xk = (act * st_s[p]).astype(bf16)
            xwk = (xk.astype(f32) * jnp.exp(ce[rows - 1:rows] - ce)).astype(bf16)
            pre_s[p] = pre_i
            x_s[p] = xk
            loc_f[p] = dot_f32(b_ref[...], xwk, ROWS)

    lane = lax.broadcasted_iota(jnp.int32, (rows, LANES), 1)

    def lanes(p):
        return pl.ds(pl.multiple_of(p * LANES, LANES), LANES)

    def mix(p):
        ce = ce_s[p]
        xp = x_s[p]
        gp = cot[:, lanes(p)]
        inner = back = None
        for i in range(per):
            gap = ce[:, i * hdim:i * hdim + 1] - cum_t[pl.ds(per * p + i, 1), :]
            m = (score_s[...] * jnp.exp(jnp.minimum(gap, 0.0))).astype(bf16)
            inner_i = dot_f32(m, xp)
            back_i = dot_f32(m, gp, ROWS)
            if inner is None:
                inner, back = inner_i, back_i
            else:
                inner = jnp.where(lane < i * hdim, inner, inner_i)
                back = jnp.where(lane < i * hdim, back, back_i)
        inner_s[p] = inner
        back_s[p] = back

    def pg_copy(p):
        slot = jnp.where(rim, 0, 1)
        return remote(pg_s.at[p], gat.at[slot, p], pg_send.at[p], pg_recv.at[slot, p],
                      seq=jnp.where(rim, d_near, d_far))

    def relay_copy(p):
        return remote(gat.at[0, p], gat.at[2, p], rl_send.at[p], pg_recv.at[2, p], seq=d_far)

    def pg_wait(slot, p):
        remote(pg_s.at[p], gat.at[slot, p], pg_send.at[p], pg_recv.at[slot, p], seq=d_far).wait_recv()

    def gradient(p):
        ce = ce_s[p]
        hi, lo = split_two(adj[p])
        bc = jnp.exp(ce[rows - 1:rows] - ce) * (dot_f32(b_ref[...], hi) + dot_f32(b_ref[...], lo))
        bc_s[p] = bc
        pre = pre_s[p]
        sig = 1.0 / (1.0 + jnp.exp(-pre))
        pg = (back_s[p] + bc) * st_s[p] * sig * (1.0 + pre * (1.0 - sig))
        pg = pg.astype(bf16).astype(f32)
        pg_s[p] = pg
        pg_t[lanes(p), :] = jnp.transpose(pg).astype(bf16)

    def by_head(value, p):
        pick = (lax.rem(lax.broadcasted_iota(jnp.int32, (2 * LANES, heads), 0), LANES) // hdim + per * p
                == lax.broadcasted_iota(jnp.int32, (2 * LANES, heads), 1)).astype(bf16)
        return dot_f32(jnp.concatenate(split_two(value), axis=1), pick)

    def output(p):
        ce = ce_s[p]
        pr, ad = prior[p], adj[p]
        grad = cot[:, lanes(p)].astype(f32)
        x = x_s[p].astype(f32)
        hi, lo = split_two(pr)
        out = inner_s[p] + jnp.exp(ce) * (dot_f32(c_ref[...], hi) + dot_f32(c_ref[...], lo))
        y_ref[:, lanes(p)] = out.astype(bf16)
        q1_s[...] += by_head(grad * out - x * back_s[p], p)
        q2_s[...] += by_head(x * bc_s[p], p)
        th_s[pl.ds(p, 1), :] = jnp.exp(ce[rows - 1:rows]) * jnp.sum(pr * ad, axis=0, keepdims=True)

    def g_copy(o):
        return remote(part.at[o], got.at[o], g_send.at[o], g_recv.at[o], head=lax.rem(h + o, nh))

    def input_part(o):
        tcols = part.shape[1]
        to = lax.rem(h + o, nh)
        part[o] = dot_f32(xw[pl.ds(pl.multiple_of(to * tcols, tcols), tcols), :], pg_t[...])
        if o:
            g_copy(o).start()

    def tk_wait(slot, q):
        remote(tk.at[slot, q], tk.at[slot, q], t_send.at[0], tk_recv.at[slot, q], seq=d_y).wait_recv()

    def core_copy(slot, i):
        q = (h, hx)[i]
        return remote(tk.at[slot, q], tk.at[slot, q], tf_send.at[slot, i], tk_recv.at[slot, q], head=hc)

    def x_copy(slot):
        return remote(tk.at[slot, h], tk.at[slot, h], tx_send.at[slot], tk_recv.at[slot, h], head=hx)

    at_row = []
    for i in range(n // 2):
        for a in range(2):
            own = y == i % 2
            on_hub = jnp.where(own, 0, 3 * unit) + a * unit
            on_rim = jnp.where(own, 2, 5) * unit if a else jnp.where(own, 6, 7) * unit
            at_row.append(jnp.where(side == 1 - i // 2, on_hub, on_rim))
    piece = math.gcd(LANES, unit)

    def build(block, source):
        for i in range(half // LANES):
            turned = jnp.transpose(source(i)).astype(bf16)
            for j in range(LANES // piece):
                r = i * LANES + j * piece
                tok_t[pl.ds(pl.multiple_of(at_row[r // unit] + r % unit, piece), piece),
                      block * rows:(block + 1) * rows] = turned[j * piece:(j + 1) * piece]

    def build_own():
        build(0, lambda i: tok[:, pl.ds(pl.multiple_of(side * half + i * LANES, LANES), LANES)].astype(f32))

    def build_from(slot):
        build(slot + 1, lambda i: tk[slot, :, :, i * LANES:(i + 1) * LANES].reshape(rows, LANES))

    def y_copy(p):
        return remote(w_oth.at[p], y_got.at[p], y_send.at[p], y_recv.at[p], seq=d_y)

    def a_copy(p):
        return remote(w_alpha.at[p], w_alpha.at[p], a_send.at[p], a_recv.at[p], seq=d_rim)

    def b_copy(p):
        return remote(w_beta.at[p], w_beta.at[p], b_send.at[p], b_recv.at[p], seq=d_rim)

    def o_copy(p):
        return remote(w_alpha.at[p, unit:], o_got.at[p], o_send.at[p], o_recv.at[p], seq=d_y)

    def weights(p):
        pg_wait(1, p)
        pg_wait(2, p)
        grads = jnp.concatenate(
            [pg_s[p].astype(bf16)] + [gat[i, p].astype(bf16) for i in range(3)], axis=0)
        w_oth[p] = dot_f32(tok_t[3 * unit:6 * unit, :], grads)
        y_copy(p).start()
        w_alpha[p] = dot_f32(tok_t[6 * unit:, :], grads)
        a_copy(p).start()
        w_own[p] = dot_f32(tok_t[:3 * unit, :], grads)

    def combine(p):
        y_copy(p).wait_recv()
        w_beta[p] = w_own[p, 2 * unit:] + y_got[p, 2 * unit:]
        b_copy(p).start()
        wg_ref[:, lanes(p)] = w_own[p, :2 * unit] + y_got[p, :2 * unit]

    def pass_on(p):
        a_copy(p).wait_recv()
        o_copy(p).start()

    def close(p):
        o_copy(p).wait_recv()
        b_copy(p).wait_recv()
        wg_ref[:unit, lanes(p)] = w_alpha[p, :unit] + o_got[p]
        wg_ref[unit:, lanes(p)] = w_beta[p]

    first = width // step_cols
    lag, early = 2, 4
    begin = jnp.maximum(lag * (n - 1 - d), first)
    rim_begin = jnp.maximum(lag * (n - 1 - d_rim), first)
    out_begin = jnp.maximum(lag * d + 1, begin) + 1
    hold = jnp.where(hub, jnp.maximum(rim_begin + 3 - early - begin, 0), 0)
    w_first, w_gap, w_rest = 18, 4, 26

    def within(k, low=0, high=pairs):
        return jnp.logical_and(k >= low, k < high)

    def slot_step(s, carry):
        at = pl.when
        kb = s - lag * (n - 1 - d)

        @at(within(kb))
        def _():
            backward(kb)

        kf = s - 1 - lag * d

        @at(within(kf))
        def _():
            forward(kf)

        @at(s == 0)
        def _():
            prepare()

        @at(s < first)
        def _():
            project(s)

        @at(within(s - first))
        def _():
            mix(s - first)

        @at(within(s - begin))
        def _():
            gradient(s - begin)

        @at(within(s - begin, 0, early))
        def _():
            pg_copy(s - begin).start()

        @at(hub)
        def _():
            relay = s - rim_begin - 3

            @at(within(relay))
            def _():
                pg_wait(0, relay)
                relay_copy(relay).start()

        @at(within(s - begin - hold, early))
        def _():
            pg_copy(s - begin - hold).start()

        @at(hub)
        def _():
            @at(s == 2)
            def _():
                build_own()

            for slot, when in ((1, 9), (2, 12)):
                @at(s == when)
                def _():
                    tk_wait(slot, h)
                    x_copy(slot).start()
                    core_copy(slot, 0).start()

                @at(s == when + 4)
                def _():
                    tk_wait(slot, hx)
                    core_copy(slot, 1).start()

                @at(s == when + 5)
                def _():
                    tk_wait(slot, hc)
                    tk_wait(slot, hxc)
                    build_from(slot)

            @at(s == 14)
            def _():
                for i in range(2):
                    tk_wait(0, (h, hx)[i])
                    core_copy(0, i).start()

            @at(s == 15)
            def _():
                tk_wait(0, hc)
                tk_wait(0, hxc)
                build_from(0)

        spaced = jnp.where(lax.rem(s - w_first + 4 * w_gap * pairs, w_gap) == 0, (s - w_first) // w_gap, -1)
        turn = jnp.where(s < w_rest, spaced, s - w_rest + (w_rest - w_first) // w_gap)

        @at(jnp.logical_and(hub, within(turn)))
        def _():
            weights(turn)

        @at(jnp.logical_and(hub, within(turn - 1)))
        def _():
            combine(turn - 1)

        @at(jnp.logical_and(rim, within(turn - 1)))
        def _():
            pass_on(turn - 1)

        @at(jnp.logical_and(rim, within(turn - 2)))
        def _():
            close(turn - 2)

        @at(within(s - out_begin))
        def _():
            output(s - out_begin)

        for o in range(nh):
            @at(s == begin + pairs + (o - 1) % nh)
            def _():
                input_part(o)

        @at(s == out_begin + pairs)
        def _():
            strict_ones = (row_ids > col_ids).astype(f32)
            which = lax.broadcasted_iota(jnp.int32, (heads, pairs), 0) // per
            row = (which == lax.broadcasted_iota(jnp.int32, (heads, pairs), 1)).astype(f32)
            mine = (lax.rem(lax.broadcasted_iota(jnp.int32, (heads, LANES), 0), per)
                    == lax.broadcasted_iota(jnp.int32, (heads, LANES), 1) // hdim)
            through = jnp.sum(jnp.where(mine, dot_exact(row, th_s[...]), 0.0), axis=1, keepdims=True)
            dg_ref[...] = (dot_exact(q1_s[...], lower_ones, ROWS)
                           + dot_exact(q2_s[...], strict_ones, (((0,), (1,)), ((), ()))) + through)

        @at(s == total_slots - 3)
        def _():
            total = part[0]
            for o in range(1, nh):
                g_copy(o).wait()
                total = total + got[o]
            tg_ref[...] = jnp.transpose(total).astype(bf16)

        return carry

    total_slots = w_rest + pairs + 2 - (w_rest - w_first) // w_gap
    lax.fori_loop(0, total_slots, slot_step, 0)

    t_far().wait_send()

    @pl.when(hub)
    def _():
        for slot in range(3):
            for i in range(2):
                core_copy(slot, i).wait_send()
            if slot:
                x_copy(slot).wait_send()

    @pl.when(rim)
    def _():
        t_near(0, h).wait_send()
        t_near(1, hx).wait_send()

    def drain(k, carry):
        @pl.when(d < n - 1)
        def _():
            fcopy(k).wait_send()

        @pl.when(d > 0)
        def _():
            bcopy(k).wait_send()

        pg_copy(k).wait_send()

        @pl.when(hub)
        def _():
            relay_copy(k).wait_send()
            y_copy(k).wait_send()
            a_copy(k).wait_send()
            b_copy(k).wait_send()

        @pl.when(rim)
        def _():
            o_copy(k).wait_send()

        return carry

    lax.fori_loop(0, pairs, drain, 0)


def hub_call(*args):
    n, nh = lax.axis_size("seq"), lax.axis_size("head")
    tokens, x_weight, b_input, _, log_decay, _, cotangent = args
    rows, width = cotangent.shape
    depth = tokens.shape[1]
    heads, state = log_decay.shape[0], b_input.shape[1]
    pairs = width // LANES
    half, unit, quarter, tcols = depth // 2, depth // (2 * n), rows // nh, depth // nh
    vm = pl.BlockSpec(memory_space=pltpu.VMEM)
    dma = pltpu.SemaphoreType.DMA
    wide = pltpu.VMEM((pairs, rows, LANES), f32)
    states = pltpu.VMEM((pairs, state, LANES), f32)

    def blocks(count):
        return pltpu.VMEM((pairs, count * unit, LANES), f32)

    scratch = [
        pltpu.VMEM((pairs, rows, LANES), bf16), wide, wide, wide, pltpu.VMEM((heads, rows), f32),
        wide, wide, wide, pltpu.VMEM((rows, rows), f32), states, states, states, states, states, states,
        pltpu.VMEM((rows, heads), f32), pltpu.VMEM((rows, heads), f32), pltpu.VMEM((pairs, LANES), f32),
        pltpu.VMEM(x_weight.shape, bf16), wide, pltpu.VMEM((width, rows), bf16),
        pltpu.VMEM((3, pairs, rows, LANES), f32), pltpu.VMEM((3, quarter, half), f32),
        pltpu.VMEM((3, nh, quarter, half), f32), pltpu.VMEM((half, 4 * rows), bf16),
        blocks(3), blocks(3), blocks(2), blocks(1), blocks(3), blocks(1),
        pltpu.VMEM((nh, tcols, rows), f32), pltpu.VMEM((nh, tcols, rows), f32),
        dma(()), dma((pairs,)), dma((pairs,)), dma((pairs,)), dma((pairs,)),
        dma((pairs,)), dma((3, pairs)), dma((pairs,)), dma((3,)), dma((3, nh)), dma((3, 2)), dma((3,)),
        dma((pairs,)), dma((pairs,)), dma((pairs,)), dma((pairs,)), dma((pairs,)), dma((pairs,)),
        dma((pairs,)), dma((pairs,)), dma((nh,)), dma((nh,))]
    outs = [jax.ShapeDtypeStruct((rows, width), bf16), jax.ShapeDtypeStruct((heads, rows), f32),
            jax.ShapeDtypeStruct((depth // n, width), f32), jax.ShapeDtypeStruct((rows, tcols), bf16)]
    return pl.pallas_call(
        functools.partial(hub_kernel, n, nh),
        out_shape=outs,
        in_specs=[vm, pl.BlockSpec(memory_space=pl.ANY)] + [vm] * (len(args) - 2),
        out_specs=[vm] * len(outs),
        scratch_shapes=scratch,
        compiler_params=pltpu.CompilerParams(
            collective_id=1, has_side_effects=True, vmem_limit_bytes=60 << 20),
        cost_estimate=pl.CostEstimate(
            flops=6 * rows * depth * width, bytes_accessed=12 << 20, transcendentals=1 << 20),
        name="hub",
    )(*args)


def hand_kernel(count, *refs):
    ins, outs, mids = refs[:count], refs[count:2 * count], refs[2 * count:3 * count]
    sems = refs[3 * count]
    first = [pltpu.make_async_copy(a, m, sems.at[0, i]) for i, (a, m) in enumerate(zip(ins, mids))]
    second = [pltpu.make_async_copy(m, b, sems.at[1, i]) for i, (m, b) in enumerate(zip(mids, outs))]
    for copy in first:
        copy.start()
    for one, two in zip(first, second):
        one.wait()
        two.start()
    for copy in second:
        copy.wait()


def hand_over(*arrays):
    anywhere = pl.BlockSpec(memory_space=pl.ANY)
    count = len(arrays)
    return pl.pallas_call(
        functools.partial(hand_kernel, count),
        out_shape=[jax.ShapeDtypeStruct(a.shape, a.dtype) for a in arrays],
        in_specs=[anywhere] * count,
        out_specs=[anywhere] * count,
        scratch_shapes=[pltpu.VMEM(a.shape, a.dtype) for a in arrays]
        + [pltpu.SemaphoreType.DMA((2, count))],
        name="hand_over",
    )(*arrays)


def per_device(tokens, x_weight, b_input, c_input, log_decay, step_size, cotangent):
    n, nh = lax.axis_size("seq"), lax.axis_size("head")
    rows, depth = tokens.shape
    assert rows == SPAN and n % 2 == 0
    args = (tokens, x_weight, b_input, c_input, log_decay.T, step_size.T, cotangent)
    if n == 8 and nh == 4:
        y, dg, wg, tg = hub_call(*args)
        y, wg, tg = hand_over(y, wg, tg)
        return y, tg, wg, dg.T
    y, pg, dg = span_call(n, *args)
    pgb = pg.astype(bf16)
    wg = lax.psum_scatter(dot_f32(tokens, pgb, ROWS), "seq", scatter_dimension=0, tiled=True)
    tg = lax.psum_scatter(dot_f32(pgb, x_weight, COLS), "head", scatter_dimension=1, tiled=True)
    return y, tg.astype(bf16), wg, dg.T


def solution(mesh):
    return jax.shard_map(
        per_device,
        mesh=mesh,
        in_specs=(
            P("seq", None),
            P(None, "head"),
            P("seq", None),
            P("seq", None),
            P("seq", "head"),
            P("seq", "head"),
            P("seq", "head"),
        ),
        out_specs=(P("seq", "head"), P("seq", "head"), P("seq", "head"), P("seq", "head")),
        check_vma=False,
    )
```

```python
import functools
import math

import jax
import jax.numpy as jnp
from jax import lax
from jax.experimental import pallas as pl
from jax.experimental.pallas import tpu as pltpu
from jax.sharding import PartitionSpec as P

SPAN = 256
LANES = 128
MESH = pl.DeviceIdType.MESH
highest = lax.Precision.HIGHEST
f32 = jnp.float32
bf16 = jnp.bfloat16


def dot_f32(a, b, dims=(((1,), (0,)), ((), ()))):
    return lax.dot_general(a, b, dims, preferred_element_type=f32)


def dot_exact(a, b, dims=(((1,), (0,)), ((), ()))):
    return lax.dot_general(a, b, dims, preferred_element_type=f32, precision=highest)


ROWS = (((0,), (0,)), ((), ()))
COLS = (((1,), (1,)), ((), ()))


def split_two(a):
    high = a.astype(bf16)
    return high, (a - high.astype(f32)).astype(bf16)


def span_kernel(n, *refs):
    tok, xw_hbm, b_ref, c_ref, ld, st, cot, y_ref, pg_ref, dg_ref = refs[:10]
    (x_s, pre_s, ce_s, st_s, cum_t, inner_s, back_s, score_s, loc_f, loc_b, out_f, out_b,
     prior, adj, q1_s, q2_s, th_s, xw, xw_sem, send_f, recv_f, send_b, recv_b) = refs[10:]
    d = lax.axis_index("seq")
    rows, width = cot.shape
    heads = ld.shape[0]
    hdim = width // heads
    pairs = width // LANES
    per = LANES // hdim
    load = pltpu.make_async_copy(xw_hbm, xw, xw_sem)
    load.start()

    barrier = pltpu.get_barrier_semaphore()
    for o in (1, n - 1):
        pl.semaphore_signal(barrier, 1, device_id={"seq": lax.rem(d + o, n)}, device_id_type=MESH)
    pl.semaphore_wait(barrier, 2)

    row_ids = lax.broadcasted_iota(jnp.int32, (rows, rows), 0)
    col_ids = lax.broadcasted_iota(jnp.int32, (rows, rows), 1)
    lower = row_ids >= col_ids
    lower_ones = lower.astype(f32)
    decay = ld[...]
    cum = dot_exact(lower_ones, decay, COLS)
    cum_t[...] = dot_exact(decay, lower_ones, COLS)
    spread = (lax.broadcasted_iota(jnp.int32, (heads, width), 0)
              == lax.broadcasted_iota(jnp.int32, (heads, width), 1) // hdim).astype(f32)
    wide_cum = dot_exact(cum, spread)
    wide_step = dot_exact(st[...], spread, ROWS)
    for p in range(pairs):
        ce_s[p] = wide_cum[:, p * LANES:(p + 1) * LANES]
        st_s[p] = wide_step[:, p * LANES:(p + 1) * LANES]
    b_val, c_val = b_ref[...], c_ref[...]
    score_s[...] = jnp.where(lower, dot_f32(c_val, b_val, COLS), 0.0)
    q1_s[...] = jnp.zeros_like(q1_s)
    q2_s[...] = jnp.zeros_like(q2_s)
    th_s[...] = jnp.zeros_like(th_s)

    load.wait()
    step_cols = 2 * LANES
    for k in range(width // step_cols):
        cols = slice(k * step_cols, (k + 1) * step_cols)
        ce = wide_cum[:, cols]
        gw = (cot[:, cols].astype(f32) * jnp.exp(ce)).astype(bf16)
        grad_k = dot_f32(c_val, gw, ROWS)
        pre = dot_f32(tok[...], xw[:, cols])
        act = pre / (1.0 + jnp.exp(-pre))
        xk = (act * wide_step[:, cols]).astype(bf16)
        xwk = (xk.astype(f32) * jnp.exp(ce[rows - 1:rows] - ce)).astype(bf16)
        state_k = dot_f32(b_val, xwk, ROWS)
        for i in range(2):
            at = slice(i * LANES, (i + 1) * LANES)
            pre_s[2 * k + i] = pre[:, at]
            x_s[2 * k + i] = xk[:, at]
            loc_b[2 * k + i] = grad_k[:, at]
            loc_f[2 * k + i] = state_k[:, at]

    @pl.when(d == 0)
    def _():
        prior[...] = jnp.zeros_like(prior)

    @pl.when(d == n - 1)
    def _():
        adj[...] = jnp.zeros_like(adj)

    def fcopy(k):
        return pltpu.make_async_remote_copy(
            src_ref=out_f.at[k], dst_ref=prior.at[k], send_sem=send_f.at[k], recv_sem=recv_f.at[k],
            device_id={"seq": lax.rem(d + 1, n)}, device_id_type=MESH)

    def bcopy(k):
        return pltpu.make_async_remote_copy(
            src_ref=out_b.at[k], dst_ref=adj.at[k], send_sem=send_b.at[k], recv_sem=recv_b.at[k],
            device_id={"seq": lax.rem(d + n - 1, n)}, device_id_type=MESH)

    lane = lax.broadcasted_iota(jnp.int32, (rows, LANES), 1)

    def mix(p):
        ce = ce_s[p]
        xp = x_s[p]
        gp = cot[:, pl.ds(pl.multiple_of(p * LANES, LANES), LANES)]
        inner = back = None
        for i in range(per):
            gap = ce[:, i * hdim:i * hdim + 1] - cum_t[pl.ds(per * p + i, 1), :]
            m = (score_s[...] * jnp.exp(jnp.minimum(gap, 0.0))).astype(bf16)
            inner_i = dot_f32(m, xp)
            back_i = dot_f32(m, gp, ROWS)
            if inner is None:
                inner, back = inner_i, back_i
            else:
                inner = jnp.where(lane < i * hdim, inner, inner_i)
                back = jnp.where(lane < i * hdim, back, back_i)
        inner_s[p] = inner
        back_s[p] = back

    def finish(p):
        ce = ce_s[p]
        end = ce[rows - 1:rows]
        at = pl.ds(pl.multiple_of(p * LANES, LANES), LANES)
        pr, ad = prior[p], adj[p]
        hi, lo = split_two(ad)
        bc = jnp.exp(end - ce) * (dot_f32(b_val, hi) + dot_f32(b_val, lo))
        bi = back_s[p]
        pre = pre_s[p]
        sig = 1.0 / (1.0 + jnp.exp(-pre))
        pg = (bi + bc) * st_s[p] * sig * (1.0 + pre * (1.0 - sig))
        pg_ref[:, at] = pg.astype(bf16).astype(f32)
        grad = cot[:, at].astype(f32)
        x = x_s[p].astype(f32)
        hi, lo = split_two(pr)
        y = inner_s[p] + jnp.exp(ce) * (dot_f32(c_val, hi) + dot_f32(c_val, lo))
        y_ref[:, at] = y.astype(bf16)
        pick = (lax.broadcasted_iota(jnp.int32, (LANES, heads), 0) // hdim + per * p
                == lax.broadcasted_iota(jnp.int32, (LANES, heads), 1)).astype(f32)
        q1_s[...] += dot_exact(grad * y - x * bi, pick)
        q2_s[...] += dot_exact(x * bc, pick)
        through = jnp.exp(end) * jnp.sum(pr * ad, axis=0, keepdims=True)
        th_s[...] += dot_exact(pick, jnp.broadcast_to(through, (8, LANES)), (((0,), (1,)), ((), ())))

    def chain(s, carry):
        kf = s - d

        @pl.when(jnp.logical_and(kf >= 0, kf < pairs))
        def _():
            @pl.when(d > 0)
            def _():
                fcopy(kf).wait_recv()

            @pl.when(d < n - 1)
            def _():
                out_f[kf] = jnp.exp(ce_s[kf, rows - 1:rows, :]) * prior[kf] + loc_f[kf]
                fcopy(kf).start()

        kb = s - (n - 1 - d)

        @pl.when(jnp.logical_and(kb >= 0, kb < pairs))
        def _():
            @pl.when(d < n - 1)
            def _():
                bcopy(kb).wait_recv()

            @pl.when(d > 0)
            def _():
                out_b[kb] = jnp.exp(ce_s[kb, rows - 1:rows, :]) * adj[kb] + loc_b[kb]
                bcopy(kb).start()

        @pl.when(s < pairs)
        def _():
            mix(s)

        ks = s - (n - 1)

        @pl.when(jnp.logical_and(ks >= 0, ks < pairs))
        def _():
            finish(ks)

        return carry

    lax.fori_loop(0, n - 1 + pairs, chain, 0)

    strict_ones = (row_ids > col_ids).astype(f32)
    dg_ref[...] = (dot_exact(q1_s[...], lower_ones, ROWS)
                   + dot_exact(q2_s[...], strict_ones, (((0,), (1,)), ((), ()))) + th_s[:, 0:1])

    @pl.when(d < n - 1)
    def _():
        def one(k, carry):
            fcopy(k).wait_send()
            return carry
        lax.fori_loop(0, pairs, one, 0)

    @pl.when(d > 0)
    def _():
        def one(k, carry):
            bcopy(k).wait_send()
            return carry
        lax.fori_loop(0, pairs, one, 0)


def span_call(n, *args):
    _, x_weight, b_input, _, log_decay, _, cotangent = args
    depth = x_weight.shape[0]
    rows, width = cotangent.shape
    heads, state = log_decay.shape[0], b_input.shape[1]
    pairs = width // LANES
    vm = pl.BlockSpec(memory_space=pltpu.VMEM)
    wide = pltpu.VMEM((pairs, rows, LANES), f32)
    states = pltpu.VMEM((pairs, state, LANES), f32)
    dma = pltpu.SemaphoreType.DMA
    scratch = [
        pltpu.VMEM((pairs, rows, LANES), bf16), wide, wide, wide, pltpu.VMEM((heads, rows), f32),
        wide, wide, pltpu.VMEM((rows, rows), f32), states, states, states, states, states, states,
        pltpu.VMEM((rows, heads), f32), pltpu.VMEM((rows, heads), f32), pltpu.VMEM((heads, 8), f32),
        pltpu.VMEM(x_weight.shape, bf16), dma(()), dma((pairs,)), dma((pairs,)), dma((pairs,)), dma((pairs,))]
    outs = [jax.ShapeDtypeStruct((rows, width), bf16), jax.ShapeDtypeStruct((rows, width), f32),
            jax.ShapeDtypeStruct((heads, rows), f32)]
    return pl.pallas_call(
        functools.partial(span_kernel, n),
        out_shape=outs,
        in_specs=[vm, pl.BlockSpec(memory_space=pl.ANY)] + [vm] * (len(args) - 2),
        out_specs=[vm] * len(outs),
        scratch_shapes=scratch,
        compiler_params=pltpu.CompilerParams(
            collective_id=0, has_side_effects=True, vmem_limit_bytes=60 << 20),
        cost_estimate=pl.CostEstimate(
            flops=6 * rows * depth * width, bytes_accessed=12 << 20, transcendentals=1 << 20),
        name="span",
    )(*args)


WINDOW = (3, 2)
RES = 3
BACK = (11, 8, 5, 2)
AHEAD = (9, 12, 15, 18)
OUT = (14, 17, 20, 23)
SEND = (14, 11, 12, 8)
RELAY = (0, 17, 12, 0)
LANE = 3
TOKENS = ((0, 1, 0), (0, 0, 0), (0, 0, 0), (10, 10, 6))
TAKE = ((17, (8, 12), (16, 19)), (19, (11, 15), (13, 17)))
BUILD = (20, 18, 21)
WSLOT = (22, 3, 28)


def hub_kernel(n, nh, *refs):
    tok_hbm, xw_hbm, b_ref, c_ref, ld, st, cot_hbm, y_ref, dg_ref, wg_ref, tg_ref = refs[:11]
    (x_s, pre_s, ce_s, st_s, cum_t, inner_s, back_s, bc_s, score_s, loc_f, loc_b, got_f, got_b, in_f, in_b, out_f, out_b,
     res_f, res_b, prior, adj,
     q1_s, q2_s, th_s, xw, tok, cot, pg_s, pg_t, gat, tsend, tk, tok_t, w_own, w_oth, w_alpha, w_beta, y_got, o_got,
     part, got, xw_sem, ch_send, ch_recv, pg_send, pg_recv, rl_send, t_send, tk_recv, tf_send,
     tx_send, y_send, y_recv, a_send, a_recv, b_send, b_recv, o_send, o_recv, g_send, g_recv) = refs[11:]
    d, h = lax.axis_index("seq"), lax.axis_index("head")
    rows, width = cot.shape
    depth = tok.shape[1]
    heads = ld.shape[0]
    hdim = width // heads
    pairs = width // LANES
    per = LANES // hdim
    quarter, half = rows // nh, depth // 2
    unit = depth // (2 * n)
    state = b_ref.shape[1]
    z, y = d // 2, lax.rem(d, 2)
    side = z // 2
    hub = jnp.logical_or(z == 1, z == 2)
    rim = jnp.logical_not(hub)
    d_near = (1 + side) * 2 + y
    d_far = (2 - side) * 2 + y
    d_rim = 3 * side * 2 + y
    d_y = d + 1 - 2 * y
    hx = lax.rem(h + 2, nh)
    hc = h + 1 - 2 * lax.rem(h, 2)
    hxc = lax.rem(hc + 2, nh)
    load_cot = pltpu.make_async_copy(cot_hbm, cot, xw_sem.at[0])
    load_tok = pltpu.make_async_copy(tok_hbm, tok, xw_sem.at[1])
    load = pltpu.make_async_copy(xw_hbm, xw, xw_sem.at[2])
    for copy in (load_cot, load_tok, load):
        copy.start()

    def remote(src, dst, send, recv, **to):
        return pltpu.make_async_remote_copy(
            src_ref=src, dst_ref=dst, send_sem=send, recv_sem=recv, device_id=to, device_id_type=MESH)

    barrier = pltpu.get_barrier_semaphore()
    for o in range(1, n):
        pl.semaphore_signal(barrier, 1, device_id={"seq": lax.rem(d + o, n)}, device_id_type=MESH)
    for o in range(1, nh):
        pl.semaphore_signal(barrier, 1, device_id={"head": lax.rem(h + o, nh)}, device_id_type=MESH)

    def token_rows(q, which):
        return tok[pl.ds(pl.multiple_of(q * quarter, quarter), quarter),
                   pl.ds(pl.multiple_of(which * half, half), half)].astype(f32)

    def t_far():
        slot = jnp.where(rim, 2, 1)
        return remote(tsend.at[2], tk.at[slot, h], t_send.at[2], tk_recv.at[slot, h], seq=d_far)

    def t_near(i, q):
        return remote(tsend.at[i], tk.at[0, q], t_send.at[i], tk_recv.at[0, q], seq=d_near)

    row_ids = lax.broadcasted_iota(jnp.int32, (rows, rows), 0)
    col_ids = lax.broadcasted_iota(jnp.int32, (rows, rows), 1)
    lower = row_ids >= col_ids
    lower_ones = lower.astype(f32)
    decay = ld[...]
    cum = dot_exact(lower_ones, decay, COLS)
    spread = (lax.broadcasted_iota(jnp.int32, (heads, width), 0)
              == lax.broadcasted_iota(jnp.int32, (heads, width), 1) // hdim).astype(f32)
    wide_cum = dot_exact(cum, spread)
    step_cols = 2 * LANES
    load_cot.wait()
    for k in range(width // step_cols):
        cols = slice(k * step_cols, (k + 1) * step_cols)
        ce = wide_cum[:, cols]
        gw = (cot[:, cols].astype(f32) * jnp.exp(ce)).astype(bf16)
        grad_k = dot_f32(c_ref[...], gw, ROWS)
        for i in range(2):
            at = slice(i * LANES, (i + 1) * LANES)
            ce_s[2 * k + i] = ce[:, at]
            loc_b[2 * k + i, :state] = grad_k[:, at]
            loc_b[2 * k + i, state:] = jnp.broadcast_to(jnp.exp(ce[rows - 1:rows, at]), (8, LANES))

    @pl.when(z == 0)
    def _():
        in_f[...] = jnp.zeros_like(in_f)

    @pl.when(z == n // 2 - 1)
    def _():
        in_b[...] = jnp.zeros_like(in_b)

    def lane_copy(kind, j):
        src, dst = ((loc_b, got_b), (loc_f, got_f))[kind]
        return remote(src.at[2 * j + 1 - y], dst.at[j], ch_send.at[kind, 0, j], ch_recv.at[kind, 0, j], seq=d_y)

    def next_copy(kind, j):
        src, dst = ((out_b, in_b), (out_f, in_f))[kind]
        to = lax.rem(d + (2 if kind else n - 2), n)
        return remote(src.at[j], dst.at[j], ch_send.at[kind, 1, j], ch_recv.at[kind, 1, j], seq=to)

    def result_copy(kind, j, p):
        src, dst = ((res_b, adj), (res_f, prior))[kind]
        return remote(src.at[j], dst.at[p], ch_send.at[kind, 2, j], ch_recv.at[kind, 2, j], seq=d_y)

    def chain(kind, j):
        p = 2 * j + y
        if kind:
            lane_copy(kind, j).wait_recv()
        begins, ends = (n // 2 - 1, 0) if kind == 0 else (0, n // 2 - 1)

        @pl.when(z != begins)
        def _():
            next_copy(kind, j).wait_recv()

        arrives = (in_b, in_f)[kind][j]
        mine, other = (loc_b[p, :state], got_b[j, :state]) if kind == 0 else (loc_f[p], got_f[j])
        my_end, other_end = loc_b[p, state:state + 1], got_b[j, state:state + 1]
        head = y == 1 - kind
        one = jnp.where(head, mine, other) + jnp.where(head, my_end, other_end) * arrives
        two = jnp.where(head, other, mine) + jnp.where(head, other_end, my_end) * one

        @pl.when(z != ends)
        def _():
            (out_b, out_f)[kind][j] = two
            next_copy(kind, j).start()

        (res_b, res_f)[kind][j] = jnp.where(head, one, arrives)
        result_copy(kind, j, p).start()
        (adj, prior)[kind][p] = jnp.where(head, arrives, one)

    def chain_result(kind, p):
        @pl.when(lax.rem(p, 2) != y)
        def _():
            result_copy(kind, p // 2, p).wait_recv()

    load_tok.wait()
    tsend[2] = token_rows(h, 1 - side)

    @pl.when(rim)
    def _():
        tsend[0] = token_rows(h, side)
        tsend[1] = token_rows(hx, side)
    pl.semaphore_wait(barrier, n + nh - 2)
    for j in range(pairs // 2):
        lane_copy(0, j).start()

    def prepare():
        cum_t[...] = dot_exact(decay, lower_ones, COLS)
        wide_step = dot_exact(st[...], spread, ROWS)
        for p in range(pairs):
            st_s[p] = wide_step[:, p * LANES:(p + 1) * LANES]
        score_s[...] = jnp.where(lower, dot_f32(c_ref[...], b_ref[...], COLS), 0.0)
        q1_s[...] = jnp.zeros_like(q1_s)
        q2_s[...] = jnp.zeros_like(q2_s)
        th_s[...] = jnp.zeros_like(th_s)
        load.wait()

    def project(k):
        pre = dot_f32(tok[...], xw[:, pl.ds(pl.multiple_of(k * step_cols, step_cols), step_cols)])
        for i in range(2):
            p = 2 * k + i
            pre_i = pre[:, i * LANES:(i + 1) * LANES]
            ce = ce_s[p]
            act = pre_i / (1.0 + jnp.exp(-pre_i))
            xk = (act * st_s[p]).astype(bf16)
            xwk = (xk.astype(f32) * jnp.exp(ce[rows - 1:rows] - ce)).astype(bf16)
            pre_s[p] = pre_i
            x_s[p] = xk
            loc_f[p] = dot_f32(b_ref[...], xwk, ROWS)

    lane = lax.broadcasted_iota(jnp.int32, (rows, LANES), 1)

    def lanes(p):
        return pl.ds(pl.multiple_of(p * LANES, LANES), LANES)

    def mix(p):
        ce = ce_s[p]
        xp = x_s[p]
        gp = cot[:, lanes(p)]
        inner = back = None
        for i in range(per):
            gap = ce[:, i * hdim:i * hdim + 1] - cum_t[pl.ds(per * p + i, 1), :]
            m = (score_s[...] * jnp.exp(jnp.minimum(gap, 0.0))).astype(bf16)
            inner_i = dot_f32(m, xp)
            back_i = dot_f32(m, gp, ROWS)
            if inner is None:
                inner, back = inner_i, back_i
            else:
                inner = jnp.where(lane < i * hdim, inner, inner_i)
                back = jnp.where(lane < i * hdim, back, back_i)
        inner_s[p] = inner
        back_s[p] = back

    def pg_copy(p):
        slot = jnp.where(rim, 0, 1)
        return remote(pg_s.at[p], gat.at[slot, p], pg_send.at[p], pg_recv.at[slot, p],
                      seq=jnp.where(rim, d_near, d_far))

    def relay_copy(p):
        return remote(gat.at[0, p], gat.at[2, p], rl_send.at[p], pg_recv.at[2, p], seq=d_far)

    def pg_wait(slot, p):
        remote(pg_s.at[p], gat.at[slot, p], pg_send.at[p], pg_recv.at[slot, p], seq=d_far).wait_recv()

    def gradient(p):
        ce = ce_s[p]
        chain_result(0, p)
        hi, lo = split_two(adj[p])
        bc = jnp.exp(ce[rows - 1:rows] - ce) * (dot_f32(b_ref[...], hi) + dot_f32(b_ref[...], lo))
        bc_s[p] = bc
        pre = pre_s[p]
        sig = 1.0 / (1.0 + jnp.exp(-pre))
        pg = (back_s[p] + bc) * st_s[p] * sig * (1.0 + pre * (1.0 - sig))
        pg = pg.astype(bf16).astype(f32)
        pg_s[p] = pg
        pg_t[lanes(p), :] = jnp.transpose(pg).astype(bf16)

    def by_head(value, p):
        pick = (lax.rem(lax.broadcasted_iota(jnp.int32, (2 * LANES, heads), 0), LANES) // hdim + per * p
                == lax.broadcasted_iota(jnp.int32, (2 * LANES, heads), 1)).astype(bf16)
        return dot_f32(jnp.concatenate(split_two(value), axis=1), pick)

    def output(p):
        chain_result(1, p)
        ce = ce_s[p]
        pr, ad = prior[p], adj[p]
        grad = cot[:, lanes(p)].astype(f32)
        x = x_s[p].astype(f32)
        hi, lo = split_two(pr)
        out = inner_s[p] + jnp.exp(ce) * (dot_f32(c_ref[...], hi) + dot_f32(c_ref[...], lo))
        y_ref[:, lanes(p)] = out.astype(bf16)
        q1_s[...] += by_head(grad * out - x * back_s[p], p)
        q2_s[...] += by_head(x * bc_s[p], p)
        th_s[pl.ds(p, 1), :] = jnp.exp(ce[rows - 1:rows]) * jnp.sum(pr * ad, axis=0, keepdims=True)

    def g_copy(o):
        return remote(part.at[o], got.at[o], g_send.at[o], g_recv.at[o], head=lax.rem(h + o, nh))

    def input_part(o):
        tcols = part.shape[1]
        to = lax.rem(h + o, nh)
        part[o] = dot_f32(xw[pl.ds(pl.multiple_of(to * tcols, tcols), tcols), :], pg_t[...])
        if o:
            g_copy(o).start()

    def tk_wait(slot, q):
        remote(tk.at[slot, q], tk.at[slot, q], t_send.at[0], tk_recv.at[slot, q], seq=d_y).wait_recv()

    def core_copy(slot, i):
        q = (h, hx)[i]
        return remote(tk.at[slot, q], tk.at[slot, q], tf_send.at[slot, i], tk_recv.at[slot, q], head=hc)

    def x_copy(slot):
        return remote(tk.at[slot, h], tk.at[slot, h], tx_send.at[slot], tk_recv.at[slot, h], head=hx)

    at_row = []
    for i in range(n // 2):
        for a in range(2):
            own = y == i % 2
            on_hub = jnp.where(own, 0, 3 * unit) + a * unit
            on_rim = jnp.where(own, 2, 5) * unit if a else jnp.where(own, 6, 7) * unit
            at_row.append(jnp.where(side == 1 - i // 2, on_hub, on_rim))
    piece = math.gcd(LANES, unit)

    def build(block, source):
        for i in range(half // LANES):
            turned = jnp.transpose(source(i)).astype(bf16)
            for j in range(LANES // piece):
                r = i * LANES + j * piece
                tok_t[pl.ds(pl.multiple_of(at_row[r // unit] + r % unit, piece), piece),
                      block * rows:(block + 1) * rows] = turned[j * piece:(j + 1) * piece]

    def build_own():
        build(0, lambda i: tok[:, pl.ds(pl.multiple_of(side * half + i * LANES, LANES), LANES)].astype(f32))

    def build_from(slot):
        build(slot + 1, lambda i: tk[slot, :, :, i * LANES:(i + 1) * LANES].reshape(rows, LANES))

    def y_copy(p):
        return remote(w_oth.at[p], y_got.at[p], y_send.at[p], y_recv.at[p], seq=d_y)

    def a_copy(p):
        return remote(w_alpha.at[p], w_alpha.at[p], a_send.at[p], a_recv.at[p], seq=d_rim)

    def b_copy(p):
        return remote(w_beta.at[p], w_beta.at[p], b_send.at[p], b_recv.at[p], seq=d_rim)

    def o_copy(p):
        return remote(w_alpha.at[p, unit:], o_got.at[p], o_send.at[p], o_recv.at[p], seq=d_y)

    def weights(p):
        pg_wait(1, p)
        pg_wait(2, p)
        grads = jnp.concatenate(
            [pg_s[p].astype(bf16)] + [gat[i, p].astype(bf16) for i in range(3)], axis=0)
        w_oth[p] = dot_f32(tok_t[3 * unit:6 * unit, :], grads)
        y_copy(p).start()
        w_alpha[p] = dot_f32(tok_t[6 * unit:, :], grads)
        a_copy(p).start()
        w_own[p] = dot_f32(tok_t[:3 * unit, :], grads)

    def combine(p):
        y_copy(p).wait_recv()
        w_beta[p] = w_own[p, 2 * unit:] + y_got[p, 2 * unit:]
        b_copy(p).start()
        wg_ref[:, lanes(p)] = w_own[p, :2 * unit] + y_got[p, :2 * unit]

    def pass_on(p):
        a_copy(p).wait_recv()
        o_copy(p).start()

    def close(p):
        o_copy(p).wait_recv()
        b_copy(p).wait_recv()
        wg_ref[:unit, lanes(p)] = w_alpha[p, :unit] + o_got[p]
        wg_ref[unit:, lanes(p)] = w_beta[p]

    first = width // step_cols
    early, follow = WINDOW

    def by_z(values):
        return jnp.where(z < 2, jnp.where(z == 0, values[0], values[1]), jnp.where(z == 2, values[2], values[3]))

    back_begin = by_z(BACK)
    begin = back_begin + RES
    ahead_begin = by_z(AHEAD)
    out_begin = by_z(OUT)
    send_begin = by_z(SEND)
    relay_begin = by_z(RELAY)
    w_first, w_gap, w_rest = WSLOT

    def within(k, low=0, high=pairs):
        return jnp.logical_and(k >= low, k < high)

    def slot_step(s, carry):
        at = pl.when
        spaced = jnp.where(lax.rem(s - w_first + 4 * w_gap * pairs, w_gap) == 0, (s - w_first) // w_gap, -1)
        turn = jnp.where(s < w_rest, spaced, s - w_rest + (w_rest - w_first) // w_gap)

        @at(within(s - min(BACK), 0, pairs // 2))
        def _():
            lane_copy(0, s - min(BACK)).wait_recv()

        @at(within(s - back_begin, 0, pairs // 2))
        def _():
            chain(0, s - back_begin)

        @at(within(s - ahead_begin, 0, pairs // 2))
        def _():
            chain(1, s - ahead_begin)

        for which, when in enumerate(TOKENS):
            for i in range(3):
                if which in (1, 2) and i < 2:
                    continue

                @at(jnp.logical_and(s == when[i], z == which))
                def _():
                    (t_far() if i == 2 else t_near(i, (h, hx)[i])).start()

        @at(s == 0)
        def _():
            prepare()

        @at(s < first)
        def _():
            project(s)

        @at(within(s - LANE, 0, pairs // 2))
        def _():
            lane_copy(1, s - LANE).start()

        @at(within(s - first))
        def _():
            mix(s - first)

        @at(within(s - begin))
        def _():
            gradient(s - begin)

        @at(within(s - send_begin, 0, jnp.where(hub, early, pairs)))
        def _():
            pg_copy(s - send_begin).start()

        relayed = jnp.where(within(s - relay_begin, 0, follow), s - relay_begin, jnp.where(turn >= 0, turn + follow, -1))

        @at(jnp.logical_and(hub, within(relayed)))
        def _():
            pg_wait(0, relayed)
            relay_copy(relayed).start()

        @at(jnp.logical_and(hub, jnp.logical_and(turn >= 0, turn + early < pairs)))
        def _():
            pg_copy(turn + early).start()

        @at(hub)
        def _():
            @at(s == 2)
            def _():
                build_own()

            for which, (near, far, rims) in ((1, TAKE[0]), (2, TAKE[1])):
                for slot, when in ((1, far), (2, rims)):
                    @at(jnp.logical_and(s == when[0], z == which))
                    def _():
                        tk_wait(slot, h)
                        x_copy(slot).start()
                        core_copy(slot, 0).start()

                    @at(jnp.logical_and(s == when[1], z == which))
                    def _():
                        tk_wait(slot, hx)
                        core_copy(slot, 1).start()

                @at(jnp.logical_and(s == near, z == which))
                def _():
                    for i in range(2):
                        tk_wait(0, (h, hx)[i])
                        core_copy(0, i).start()

            for slot in range(3):
                @at(s == BUILD[slot])
                def _():
                    tk_wait(slot, hc)
                    tk_wait(slot, hxc)
                    build_from(slot)

        @at(jnp.logical_and(hub, within(turn)))
        def _():
            weights(turn)

        @at(jnp.logical_and(hub, within(turn - 1)))
        def _():
            combine(turn - 1)

        @at(jnp.logical_and(rim, within(turn - 1)))
        def _():
            pass_on(turn - 1)

        @at(jnp.logical_and(rim, within(turn - 2)))
        def _():
            close(turn - 2)

        @at(within(s - out_begin))
        def _():
            output(s - out_begin)

        for o in range(nh):
            @at(s == begin + pairs + (o - 1) % nh)
            def _():
                input_part(o)

        @at(s == out_begin + pairs)
        def _():
            strict_ones = (row_ids > col_ids).astype(f32)
            which = lax.broadcasted_iota(jnp.int32, (heads, pairs), 0) // per
            row = (which == lax.broadcasted_iota(jnp.int32, (heads, pairs), 1)).astype(f32)
            mine = (lax.rem(lax.broadcasted_iota(jnp.int32, (heads, LANES), 0), per)
                    == lax.broadcasted_iota(jnp.int32, (heads, LANES), 1) // hdim)
            through = jnp.sum(jnp.where(mine, dot_exact(row, th_s[...]), 0.0), axis=1, keepdims=True)
            dg_ref[...] = (dot_exact(q1_s[...], lower_ones, ROWS)
                           + dot_exact(q2_s[...], strict_ones, (((0,), (1,)), ((), ()))) + through)

        @at(s == total_slots - 3)
        def _():
            total = part[0]
            for o in range(1, nh):
                g_copy(o).wait()
                total = total + got[o]
            tg_ref[...] = jnp.transpose(total).astype(bf16)

        return carry

    total_slots = w_rest + pairs + 2 - (w_rest - w_first) // w_gap
    lax.fori_loop(0, total_slots, slot_step, 0)

    t_far().wait_send()

    @pl.when(hub)
    def _():
        for slot in range(3):
            for i in range(2):
                core_copy(slot, i).wait_send()
            if slot:
                x_copy(slot).wait_send()

    @pl.when(rim)
    def _():
        t_near(0, h).wait_send()
        t_near(1, hx).wait_send()

    def drain(k, carry):
        @pl.when(k < pairs // 2)
        def _():
            for kind in range(2):
                lane_copy(kind, k).wait_send()
                result_copy(kind, k, 2 * k + y).wait_send()

                @pl.when(z != (0, n // 2 - 1)[kind])
                def _():
                    next_copy(kind, k).wait_send()

        pg_copy(k).wait_send()

        @pl.when(hub)
        def _():
            relay_copy(k).wait_send()
            y_copy(k).wait_send()
            a_copy(k).wait_send()
            b_copy(k).wait_send()

        @pl.when(rim)
        def _():
            o_copy(k).wait_send()

        return carry

    lax.fori_loop(0, pairs, drain, 0)


def hub_call(*args):
    n, nh = lax.axis_size("seq"), lax.axis_size("head")
    tokens, x_weight, b_input, _, log_decay, _, cotangent = args
    rows, width = cotangent.shape
    depth = tokens.shape[1]
    heads, state = log_decay.shape[0], b_input.shape[1]
    pairs = width // LANES
    half, unit, quarter, tcols = depth // 2, depth // (2 * n), rows // nh, depth // nh
    vm = pl.BlockSpec(memory_space=pltpu.VMEM)
    anywhere = pl.BlockSpec(memory_space=pl.ANY)
    dma = pltpu.SemaphoreType.DMA
    wide = pltpu.VMEM((pairs, rows, LANES), f32)

    def states(more=0, split=1):
        return pltpu.VMEM((pairs // split, state + more, LANES), f32)

    def blocks(count):
        return pltpu.VMEM((pairs, count * unit, LANES), f32)

    scratch = [
        pltpu.VMEM((pairs, rows, LANES), bf16), wide, wide, wide, pltpu.VMEM((heads, rows), f32),
        wide, wide, wide, pltpu.VMEM((rows, rows), f32), states(), states(8), states(0, 2), states(8, 2),
        states(0, 2), states(0, 2), states(0, 2), states(0, 2), states(0, 2), states(0, 2), states(), states(),
        pltpu.VMEM((rows, heads), f32), pltpu.VMEM((rows, heads), f32), pltpu.VMEM((pairs, LANES), f32),
        pltpu.VMEM(x_weight.shape, bf16), pltpu.VMEM(tokens.shape, bf16), pltpu.VMEM(cotangent.shape, bf16),
        wide, pltpu.VMEM((width, rows), bf16),
        pltpu.VMEM((3, pairs, rows, LANES), f32), pltpu.VMEM((3, quarter, half), f32),
        pltpu.VMEM((3, nh, quarter, half), f32), pltpu.VMEM((half, 4 * rows), bf16),
        blocks(3), blocks(3), blocks(2), blocks(1), blocks(3), blocks(1),
        pltpu.VMEM((nh, tcols, rows), f32), pltpu.VMEM((nh, tcols, rows), f32),
        dma((3,)), dma((2, 3, pairs // 2)), dma((2, 3, pairs // 2)),
        dma((pairs,)), dma((3, pairs)), dma((pairs,)), dma((3,)), dma((3, nh)), dma((3, 2)), dma((3,)),
        dma((pairs,)), dma((pairs,)), dma((pairs,)), dma((pairs,)), dma((pairs,)), dma((pairs,)),
        dma((pairs,)), dma((pairs,)), dma((nh,)), dma((nh,))]
    outs = [jax.ShapeDtypeStruct((rows, width), bf16), jax.ShapeDtypeStruct((heads, rows), f32),
            jax.ShapeDtypeStruct((depth // n, width), f32), jax.ShapeDtypeStruct((rows, tcols), bf16)]
    return pl.pallas_call(
        functools.partial(hub_kernel, n, nh),
        out_shape=outs,
        in_specs=[anywhere] * 2 + [vm] * 4 + [anywhere],
        out_specs=[vm] * len(outs),
        scratch_shapes=scratch,
        compiler_params=pltpu.CompilerParams(
            collective_id=1, has_side_effects=True, vmem_limit_bytes=60 << 20),
        cost_estimate=pl.CostEstimate(
            flops=6 * rows * depth * width, bytes_accessed=12 << 20, transcendentals=1 << 20),
        name="hub",
    )(*args)


def hand_kernel(count, *refs):
    ins, outs, mids = refs[:count], refs[count:2 * count], refs[2 * count:3 * count]
    sems = refs[3 * count]
    first = [pltpu.make_async_copy(a, m, sems.at[0, i]) for i, (a, m) in enumerate(zip(ins, mids))]
    second = [pltpu.make_async_copy(m, b, sems.at[1, i]) for i, (m, b) in enumerate(zip(mids, outs))]
    for copy in first:
        copy.start()
    for one, two in zip(first, second):
        one.wait()
        two.start()
    for copy in second:
        copy.wait()


def hand_over(*arrays):
    anywhere = pl.BlockSpec(memory_space=pl.ANY)
    count = len(arrays)
    return pl.pallas_call(
        functools.partial(hand_kernel, count),
        out_shape=[jax.ShapeDtypeStruct(a.shape, a.dtype) for a in arrays],
        in_specs=[anywhere] * count,
        out_specs=[anywhere] * count,
        scratch_shapes=[pltpu.VMEM(a.shape, a.dtype) for a in arrays]
        + [pltpu.SemaphoreType.DMA((2, count))],
        name="hand_over",
    )(*arrays)


def per_device(tokens, x_weight, b_input, c_input, log_decay, step_size, cotangent):
    n, nh = lax.axis_size("seq"), lax.axis_size("head")
    rows, depth = tokens.shape
    assert rows == SPAN and n % 2 == 0
    args = (tokens, x_weight, b_input, c_input, log_decay.T, step_size.T, cotangent)
    if n == 8 and nh == 4:
        y, dg, wg, tg = hub_call(*args)
        y, wg, tg = hand_over(y, wg, tg)
        return y, tg, wg, dg.T
    y, pg, dg = span_call(n, *args)
    pgb = pg.astype(bf16)
    wg = lax.psum_scatter(dot_f32(tokens, pgb, ROWS), "seq", scatter_dimension=0, tiled=True)
    tg = lax.psum_scatter(dot_f32(pgb, x_weight, COLS), "head", scatter_dimension=1, tiled=True)
    return y, tg.astype(bf16), wg, dg.T


def solution(mesh):
    return jax.shard_map(
        per_device,
        mesh=mesh,
        in_specs=(
            P("seq", None),
            P(None, "head"),
            P("seq", None),
            P("seq", None),
            P("seq", "head"),
            P("seq", "head"),
            P("seq", "head"),
        ),
        out_specs=(P("seq", "head"), P("seq", "head"), P("seq", "head"), P("seq", "head")),
        check_vma=False,
    )
```

```python
import functools
import math

import jax
import jax.numpy as jnp
from jax import lax
from jax.experimental import pallas as pl
from jax.experimental.pallas import tpu as pltpu
from jax.sharding import PartitionSpec as P

SPAN = 256
LANES = 128
MESH = pl.DeviceIdType.MESH
highest = lax.Precision.HIGHEST
f32 = jnp.float32
bf16 = jnp.bfloat16


def dot_f32(a, b, dims=(((1,), (0,)), ((), ()))):
    return lax.dot_general(a, b, dims, preferred_element_type=f32)


def dot_exact(a, b, dims=(((1,), (0,)), ((), ()))):
    return lax.dot_general(a, b, dims, preferred_element_type=f32, precision=highest)


ROWS = (((0,), (0,)), ((), ()))
COLS = (((1,), (1,)), ((), ()))


def split_two(a):
    high = a.astype(bf16)
    return high, (a - high.astype(f32)).astype(bf16)


def span_kernel(n, *refs):
    tok, xw_hbm, b_ref, c_ref, ld, st, cot, y_ref, pg_ref, dg_ref = refs[:10]
    (x_s, pre_s, ce_s, st_s, cum_t, inner_s, back_s, score_s, loc_f, loc_b, out_f, out_b,
     prior, adj, q1_s, q2_s, th_s, xw, xw_sem, send_f, recv_f, send_b, recv_b) = refs[10:]
    d = lax.axis_index("seq")
    rows, width = cot.shape
    heads = ld.shape[0]
    hdim = width // heads
    pairs = width // LANES
    per = LANES // hdim
    load = pltpu.make_async_copy(xw_hbm, xw, xw_sem)
    load.start()

    barrier = pltpu.get_barrier_semaphore()
    for o in (1, n - 1):
        pl.semaphore_signal(barrier, 1, device_id={"seq": lax.rem(d + o, n)}, device_id_type=MESH)
    pl.semaphore_wait(barrier, 2)

    row_ids = lax.broadcasted_iota(jnp.int32, (rows, rows), 0)
    col_ids = lax.broadcasted_iota(jnp.int32, (rows, rows), 1)
    lower = row_ids >= col_ids
    lower_ones = lower.astype(f32)
    decay = ld[...]
    cum = dot_exact(lower_ones, decay, COLS)
    cum_t[...] = dot_exact(decay, lower_ones, COLS)
    spread = (lax.broadcasted_iota(jnp.int32, (heads, width), 0)
              == lax.broadcasted_iota(jnp.int32, (heads, width), 1) // hdim).astype(f32)
    wide_cum = dot_exact(cum, spread)
    wide_step = dot_exact(st[...], spread, ROWS)
    for p in range(pairs):
        ce_s[p] = wide_cum[:, p * LANES:(p + 1) * LANES]
        st_s[p] = wide_step[:, p * LANES:(p + 1) * LANES]
    b_val, c_val = b_ref[...], c_ref[...]
    score_s[...] = jnp.where(lower, dot_f32(c_val, b_val, COLS), 0.0)
    q1_s[...] = jnp.zeros_like(q1_s)
    q2_s[...] = jnp.zeros_like(q2_s)
    th_s[...] = jnp.zeros_like(th_s)

    load.wait()
    step_cols = 2 * LANES
    for k in range(width // step_cols):
        cols = slice(k * step_cols, (k + 1) * step_cols)
        ce = wide_cum[:, cols]
        gw = (cot[:, cols].astype(f32) * jnp.exp(ce)).astype(bf16)
        grad_k = dot_f32(c_val, gw, ROWS)
        pre = dot_f32(tok[...], xw[:, cols])
        act = pre / (1.0 + jnp.exp(-pre))
        xk = (act * wide_step[:, cols]).astype(bf16)
        xwk = (xk.astype(f32) * jnp.exp(ce[rows - 1:rows] - ce)).astype(bf16)
        state_k = dot_f32(b_val, xwk, ROWS)
        for i in range(2):
            at = slice(i * LANES, (i + 1) * LANES)
            pre_s[2 * k + i] = pre[:, at]
            x_s[2 * k + i] = xk[:, at]
            loc_b[2 * k + i] = grad_k[:, at]
            loc_f[2 * k + i] = state_k[:, at]

    @pl.when(d == 0)
    def _():
        prior[...] = jnp.zeros_like(prior)

    @pl.when(d == n - 1)
    def _():
        adj[...] = jnp.zeros_like(adj)

    def fcopy(k):
        return pltpu.make_async_remote_copy(
            src_ref=out_f.at[k], dst_ref=prior.at[k], send_sem=send_f.at[k], recv_sem=recv_f.at[k],
            device_id={"seq": lax.rem(d + 1, n)}, device_id_type=MESH)

    def bcopy(k):
        return pltpu.make_async_remote_copy(
            src_ref=out_b.at[k], dst_ref=adj.at[k], send_sem=send_b.at[k], recv_sem=recv_b.at[k],
            device_id={"seq": lax.rem(d + n - 1, n)}, device_id_type=MESH)

    lane = lax.broadcasted_iota(jnp.int32, (rows, LANES), 1)

    def mix(p):
        ce = ce_s[p]
        xp = x_s[p]
        gp = cot[:, pl.ds(pl.multiple_of(p * LANES, LANES), LANES)]
        inner = back = None
        for i in range(per):
            gap = ce[:, i * hdim:i * hdim + 1] - cum_t[pl.ds(per * p + i, 1), :]
            m = (score_s[...] * jnp.exp(jnp.minimum(gap, 0.0))).astype(bf16)
            inner_i = dot_f32(m, xp)
            back_i = dot_f32(m, gp, ROWS)
            if inner is None:
                inner, back = inner_i, back_i
            else:
                inner = jnp.where(lane < i * hdim, inner, inner_i)
                back = jnp.where(lane < i * hdim, back, back_i)
        inner_s[p] = inner
        back_s[p] = back

    def finish(p):
        ce = ce_s[p]
        end = ce[rows - 1:rows]
        at = pl.ds(pl.multiple_of(p * LANES, LANES), LANES)
        pr, ad = prior[p], adj[p]
        hi, lo = split_two(ad)
        bc = jnp.exp(end - ce) * (dot_f32(b_val, hi) + dot_f32(b_val, lo))
        bi = back_s[p]
        pre = pre_s[p]
        sig = 1.0 / (1.0 + jnp.exp(-pre))
        pg = (bi + bc) * st_s[p] * sig * (1.0 + pre * (1.0 - sig))
        pg_ref[:, at] = pg.astype(bf16).astype(f32)
        grad = cot[:, at].astype(f32)
        x = x_s[p].astype(f32)
        hi, lo = split_two(pr)
        y = inner_s[p] + jnp.exp(ce) * (dot_f32(c_val, hi) + dot_f32(c_val, lo))
        y_ref[:, at] = y.astype(bf16)
        pick = (lax.broadcasted_iota(jnp.int32, (LANES, heads), 0) // hdim + per * p
                == lax.broadcasted_iota(jnp.int32, (LANES, heads), 1)).astype(f32)
        q1_s[...] += dot_exact(grad * y - x * bi, pick)
        q2_s[...] += dot_exact(x * bc, pick)
        through = jnp.exp(end) * jnp.sum(pr * ad, axis=0, keepdims=True)
        th_s[...] += dot_exact(pick, jnp.broadcast_to(through, (8, LANES)), (((0,), (1,)), ((), ())))

    def chain(s, carry):
        kf = s - d

        @pl.when(jnp.logical_and(kf >= 0, kf < pairs))
        def _():
            @pl.when(d > 0)
            def _():
                fcopy(kf).wait_recv()

            @pl.when(d < n - 1)
            def _():
                out_f[kf] = jnp.exp(ce_s[kf, rows - 1:rows, :]) * prior[kf] + loc_f[kf]
                fcopy(kf).start()

        kb = s - (n - 1 - d)

        @pl.when(jnp.logical_and(kb >= 0, kb < pairs))
        def _():
            @pl.when(d < n - 1)
            def _():
                bcopy(kb).wait_recv()

            @pl.when(d > 0)
            def _():
                out_b[kb] = jnp.exp(ce_s[kb, rows - 1:rows, :]) * adj[kb] + loc_b[kb]
                bcopy(kb).start()

        @pl.when(s < pairs)
        def _():
            mix(s)

        ks = s - (n - 1)

        @pl.when(jnp.logical_and(ks >= 0, ks < pairs))
        def _():
            finish(ks)

        return carry

    lax.fori_loop(0, n - 1 + pairs, chain, 0)

    strict_ones = (row_ids > col_ids).astype(f32)
    dg_ref[...] = (dot_exact(q1_s[...], lower_ones, ROWS)
                   + dot_exact(q2_s[...], strict_ones, (((0,), (1,)), ((), ()))) + th_s[:, 0:1])

    @pl.when(d < n - 1)
    def _():
        def one(k, carry):
            fcopy(k).wait_send()
            return carry
        lax.fori_loop(0, pairs, one, 0)

    @pl.when(d > 0)
    def _():
        def one(k, carry):
            bcopy(k).wait_send()
            return carry
        lax.fori_loop(0, pairs, one, 0)


def span_call(n, *args):
    _, x_weight, b_input, _, log_decay, _, cotangent = args
    depth = x_weight.shape[0]
    rows, width = cotangent.shape
    heads, state = log_decay.shape[0], b_input.shape[1]
    pairs = width // LANES
    vm = pl.BlockSpec(memory_space=pltpu.VMEM)
    wide = pltpu.VMEM((pairs, rows, LANES), f32)
    states = pltpu.VMEM((pairs, state, LANES), f32)
    dma = pltpu.SemaphoreType.DMA
    scratch = [
        pltpu.VMEM((pairs, rows, LANES), bf16), wide, wide, wide, pltpu.VMEM((heads, rows), f32),
        wide, wide, pltpu.VMEM((rows, rows), f32), states, states, states, states, states, states,
        pltpu.VMEM((rows, heads), f32), pltpu.VMEM((rows, heads), f32), pltpu.VMEM((heads, 8), f32),
        pltpu.VMEM(x_weight.shape, bf16), dma(()), dma((pairs,)), dma((pairs,)), dma((pairs,)), dma((pairs,))]
    outs = [jax.ShapeDtypeStruct((rows, width), bf16), jax.ShapeDtypeStruct((rows, width), f32),
            jax.ShapeDtypeStruct((heads, rows), f32)]
    return pl.pallas_call(
        functools.partial(span_kernel, n),
        out_shape=outs,
        in_specs=[vm, pl.BlockSpec(memory_space=pl.ANY)] + [vm] * (len(args) - 2),
        out_specs=[vm] * len(outs),
        scratch_shapes=scratch,
        compiler_params=pltpu.CompilerParams(
            collective_id=0, has_side_effects=True, vmem_limit_bytes=60 << 20),
        cost_estimate=pl.CostEstimate(
            flops=6 * rows * depth * width, bytes_accessed=12 << 20, transcendentals=1 << 20),
        name="span",
    )(*args)


WINDOW = (3, 2)
RES = 3
BACK = (11, 8, 5, 2)
AHEAD = (9, 12, 15, 18)
OUT = (14, 24, 24, 23)
SEND = (14, 11, 12, 8)
RELAY = (0, 17, 12, 0)
LANE = 3
TG = (24, 25, 25, 18)
TOKENS = ((0, 1, 0), (0, 0, 0), (0, 0, 0), (10, 10, 6))
TAKE = ((17, (8, 12), (16, 19)), (19, (11, 15), (13, 17)))
BUILD = (20, 18, 21)
WSLOT = (21, 2, 25)


def hub_kernel(n, nh, *refs):
    tok_hbm, xw_hbm, b_ref, c_ref, ld, st, cot_hbm, y_ref, dg_ref, wg_ref, tg_ref = refs[:11]
    (x_s, pre_s, ce_s, st_s, cum_t, inner_s, back_s, bc_s, score_s, loc_f, loc_b, got_f, got_b, in_f, in_b, out_f, out_b,
     res_f, res_b, prior, adj,
     q1_s, q2_s, th_s, xw, tok, cot, pg_s, pg_t, gat, tsend, tk, tok_t, w_own, w_oth, w_alpha, w_beta, y_got, o_got,
     part, got, xw_sem, ch_send, ch_recv, pg_send, pg_recv, rl_send, t_send, tk_recv, tf_send,
     tx_send, y_send, y_recv, a_send, a_recv, b_send, b_recv, o_send, o_recv, g_send, g_recv) = refs[11:]
    d, h = lax.axis_index("seq"), lax.axis_index("head")
    rows, width = cot.shape
    depth = tok.shape[1]
    heads = ld.shape[0]
    hdim = width // heads
    pairs = width // LANES
    per = LANES // hdim
    quarter, half = rows // nh, depth // 2
    unit = depth // (2 * n)
    state = b_ref.shape[1]
    z, y = d // 2, lax.rem(d, 2)
    side = z // 2
    hub = jnp.logical_or(z == 1, z == 2)
    rim = jnp.logical_not(hub)
    d_near = (1 + side) * 2 + y
    d_far = (2 - side) * 2 + y
    d_rim = 3 * side * 2 + y
    d_y = d + 1 - 2 * y
    hx = lax.rem(h + 2, nh)
    hc = h + 1 - 2 * lax.rem(h, 2)
    hxc = lax.rem(hc + 2, nh)
    load_cot = pltpu.make_async_copy(cot_hbm, cot, xw_sem.at[0])
    load_tok = pltpu.make_async_copy(tok_hbm, tok, xw_sem.at[1])
    load = pltpu.make_async_copy(xw_hbm, xw, xw_sem.at[2])
    for copy in (load_cot, load_tok, load):
        copy.start()

    def remote(src, dst, send, recv, **to):
        return pltpu.make_async_remote_copy(
            src_ref=src, dst_ref=dst, send_sem=send, recv_sem=recv, device_id=to, device_id_type=MESH)

    barrier = pltpu.get_barrier_semaphore()
    for o in range(1, n):
        pl.semaphore_signal(barrier, 1, device_id={"seq": lax.rem(d + o, n)}, device_id_type=MESH)
    for o in range(1, nh):
        pl.semaphore_signal(barrier, 1, device_id={"head": lax.rem(h + o, nh)}, device_id_type=MESH)

    def token_rows(q, which):
        return tok[pl.ds(pl.multiple_of(q * quarter, quarter), quarter),
                   pl.ds(pl.multiple_of(which * half, half), half)].astype(f32)

    def t_far():
        slot = jnp.where(rim, 2, 1)
        return remote(tsend.at[2], tk.at[slot, h], t_send.at[2], tk_recv.at[slot, h], seq=d_far)

    def t_near(i, q):
        return remote(tsend.at[i], tk.at[0, q], t_send.at[i], tk_recv.at[0, q], seq=d_near)

    row_ids = lax.broadcasted_iota(jnp.int32, (rows, rows), 0)
    col_ids = lax.broadcasted_iota(jnp.int32, (rows, rows), 1)
    lower = row_ids >= col_ids
    lower_ones = lower.astype(f32)
    decay = ld[...]
    cum = dot_exact(lower_ones, decay, COLS)
    spread = (lax.broadcasted_iota(jnp.int32, (heads, width), 0)
              == lax.broadcasted_iota(jnp.int32, (heads, width), 1) // hdim).astype(f32)
    wide_cum = dot_exact(cum, spread)
    step_cols = 2 * LANES
    load_cot.wait()
    for k in range(width // step_cols):
        cols = slice(k * step_cols, (k + 1) * step_cols)
        ce = wide_cum[:, cols]
        gw = (cot[:, cols].astype(f32) * jnp.exp(ce)).astype(bf16)
        grad_k = dot_f32(c_ref[...], gw, ROWS)
        for i in range(2):
            at = slice(i * LANES, (i + 1) * LANES)
            ce_s[2 * k + i] = ce[:, at]
            loc_b[2 * k + i, :state] = grad_k[:, at]
            loc_b[2 * k + i, state:] = jnp.broadcast_to(jnp.exp(ce[rows - 1:rows, at]), (8, LANES))

    @pl.when(z == 0)
    def _():
        in_f[...] = jnp.zeros_like(in_f)

    @pl.when(z == n // 2 - 1)
    def _():
        in_b[...] = jnp.zeros_like(in_b)

    def lane_copy(kind, j):
        src, dst = ((loc_b, got_b), (loc_f, got_f))[kind]
        return remote(src.at[2 * j + 1 - y], dst.at[j], ch_send.at[kind, 0, j], ch_recv.at[kind, 0, j], seq=d_y)

    def next_copy(kind, j):
        src, dst = ((out_b, in_b), (out_f, in_f))[kind]
        to = lax.rem(d + (2 if kind else n - 2), n)
        return remote(src.at[j], dst.at[j], ch_send.at[kind, 1, j], ch_recv.at[kind, 1, j], seq=to)

    def result_copy(kind, j, p):
        src, dst = ((res_b, adj), (res_f, prior))[kind]
        return remote(src.at[j], dst.at[p], ch_send.at[kind, 2, j], ch_recv.at[kind, 2, j], seq=d_y)

    def chain(kind, j):
        p = 2 * j + y
        if kind:
            lane_copy(kind, j).wait_recv()
        begins, ends = (n // 2 - 1, 0) if kind == 0 else (0, n // 2 - 1)

        @pl.when(z != begins)
        def _():
            next_copy(kind, j).wait_recv()

        arrives = (in_b, in_f)[kind][j]
        mine, other = (loc_b[p, :state], got_b[j, :state]) if kind == 0 else (loc_f[p], got_f[j])
        my_end, other_end = loc_b[p, state:state + 1], got_b[j, state:state + 1]
        head = y == 1 - kind
        one = jnp.where(head, mine, other) + jnp.where(head, my_end, other_end) * arrives
        two = jnp.where(head, other, mine) + jnp.where(head, other_end, my_end) * one

        @pl.when(z != ends)
        def _():
            (out_b, out_f)[kind][j] = two
            next_copy(kind, j).start()

        (res_b, res_f)[kind][j] = jnp.where(head, one, arrives)
        result_copy(kind, j, p).start()
        (adj, prior)[kind][p] = jnp.where(head, arrives, one)

    def chain_result(kind, p):
        @pl.when(lax.rem(p, 2) != y)
        def _():
            result_copy(kind, p // 2, p).wait_recv()

    load_tok.wait()
    tsend[2] = token_rows(h, 1 - side)

    @pl.when(rim)
    def _():
        tsend[0] = token_rows(h, side)
        tsend[1] = token_rows(hx, side)
    pl.semaphore_wait(barrier, n + nh - 2)
    for j in range(pairs // 2):
        lane_copy(0, j).start()

    def prepare():
        cum_t[...] = dot_exact(decay, lower_ones, COLS)
        wide_step = dot_exact(st[...], spread, ROWS)
        for p in range(pairs):
            st_s[p] = wide_step[:, p * LANES:(p + 1) * LANES]
        score_s[...] = jnp.where(lower, dot_f32(c_ref[...], b_ref[...], COLS), 0.0)
        q1_s[...] = jnp.zeros_like(q1_s)
        q2_s[...] = jnp.zeros_like(q2_s)
        th_s[...] = jnp.zeros_like(th_s)
        load.wait()

    def project(k):
        pre = dot_f32(tok[...], xw[:, pl.ds(pl.multiple_of(k * step_cols, step_cols), step_cols)])
        for i in range(2):
            p = 2 * k + i
            pre_i = pre[:, i * LANES:(i + 1) * LANES]
            ce = ce_s[p]
            act = pre_i / (1.0 + jnp.exp(-pre_i))
            xk = (act * st_s[p]).astype(bf16)
            xwk = (xk.astype(f32) * jnp.exp(ce[rows - 1:rows] - ce)).astype(bf16)
            pre_s[p] = pre_i
            x_s[p] = xk
            loc_f[p] = dot_f32(b_ref[...], xwk, ROWS)

    lane = lax.broadcasted_iota(jnp.int32, (rows, LANES), 1)

    def lanes(p):
        return pl.ds(pl.multiple_of(p * LANES, LANES), LANES)

    def mix(p):
        ce = ce_s[p]
        xp = x_s[p]
        gp = cot[:, lanes(p)]
        inner = back = None
        for i in range(per):
            gap = ce[:, i * hdim:i * hdim + 1] - cum_t[pl.ds(per * p + i, 1), :]
            m = (score_s[...] * jnp.exp(jnp.minimum(gap, 0.0))).astype(bf16)
            inner_i = dot_f32(m, xp)
            back_i = dot_f32(m, gp, ROWS)
            if inner is None:
                inner, back = inner_i, back_i
            else:
                inner = jnp.where(lane < i * hdim, inner, inner_i)
                back = jnp.where(lane < i * hdim, back, back_i)
        inner_s[p] = inner
        back_s[p] = back

    def pg_copy(p):
        slot = jnp.where(rim, 0, 1)
        return remote(pg_s.at[p], gat.at[slot, p], pg_send.at[p], pg_recv.at[slot, p],
                      seq=jnp.where(rim, d_near, d_far))

    def relay_copy(p):
        return remote(gat.at[0, p], gat.at[2, p], rl_send.at[p], pg_recv.at[2, p], seq=d_far)

    def pg_wait(slot, p):
        remote(pg_s.at[p], gat.at[slot, p], pg_send.at[p], pg_recv.at[slot, p], seq=d_far).wait_recv()

    def gradient(p):
        ce = ce_s[p]
        chain_result(0, p)
        hi, lo = split_two(adj[p])
        bc = jnp.exp(ce[rows - 1:rows] - ce) * (dot_f32(b_ref[...], hi) + dot_f32(b_ref[...], lo))
        bc_s[p] = bc
        pre = pre_s[p]
        sig = 1.0 / (1.0 + jnp.exp(-pre))
        pg = (back_s[p] + bc) * st_s[p] * sig * (1.0 + pre * (1.0 - sig))
        pg = pg.astype(bf16).astype(f32)
        pg_s[p] = pg
        pg_t[lanes(p), :] = jnp.transpose(pg).astype(bf16)

    def by_head(value, p):
        pick = (lax.rem(lax.broadcasted_iota(jnp.int32, (2 * LANES, heads), 0), LANES) // hdim + per * p
                == lax.broadcasted_iota(jnp.int32, (2 * LANES, heads), 1)).astype(bf16)
        return dot_f32(jnp.concatenate(split_two(value), axis=1), pick)

    def output(p):
        chain_result(1, p)
        ce = ce_s[p]
        pr, ad = prior[p], adj[p]
        grad = cot[:, lanes(p)].astype(f32)
        x = x_s[p].astype(f32)
        hi, lo = split_two(pr)
        out = inner_s[p] + jnp.exp(ce) * (dot_f32(c_ref[...], hi) + dot_f32(c_ref[...], lo))
        y_ref[:, lanes(p)] = out.astype(bf16)
        q1_s[...] += by_head(grad * out - x * back_s[p], p)
        q2_s[...] += by_head(x * bc_s[p], p)
        th_s[pl.ds(p, 1), :] = jnp.exp(ce[rows - 1:rows]) * jnp.sum(pr * ad, axis=0, keepdims=True)

    def g_copy(o):
        return remote(part.at[o], got.at[o], g_send.at[o], g_recv.at[o], head=lax.rem(h + o, nh))

    def input_part(o):
        tcols = part.shape[1]
        to = lax.rem(h + o, nh)
        part[o] = dot_f32(xw[pl.ds(pl.multiple_of(to * tcols, tcols), tcols), :], pg_t[...])
        if o:
            g_copy(o).start()

    def tk_wait(slot, q):
        remote(tk.at[slot, q], tk.at[slot, q], t_send.at[0], tk_recv.at[slot, q], seq=d_y).wait_recv()

    def core_copy(slot, i):
        q = (h, hx)[i]
        return remote(tk.at[slot, q], tk.at[slot, q], tf_send.at[slot, i], tk_recv.at[slot, q], head=hc)

    def x_copy(slot):
        return remote(tk.at[slot, h], tk.at[slot, h], tx_send.at[slot], tk_recv.at[slot, h], head=hx)

    at_row = []
    for i in range(n // 2):
        for a in range(2):
            own = y == i % 2
            on_hub = jnp.where(own, 0, 3 * unit) + a * unit
            on_rim = jnp.where(own, 2, 5) * unit if a else jnp.where(own, 6, 7) * unit
            at_row.append(jnp.where(side == 1 - i // 2, on_hub, on_rim))
    piece = math.gcd(LANES, unit)

    def build(block, source):
        for i in range(half // LANES):
            turned = jnp.transpose(source(i)).astype(bf16)
            for j in range(LANES // piece):
                r = i * LANES + j * piece
                tok_t[pl.ds(pl.multiple_of(at_row[r // unit] + r % unit, piece), piece),
                      block * rows:(block + 1) * rows] = turned[j * piece:(j + 1) * piece]

    def build_own():
        build(0, lambda i: tok[:, pl.ds(pl.multiple_of(side * half + i * LANES, LANES), LANES)].astype(f32))

    def build_from(slot):
        build(slot + 1, lambda i: tk[slot, :, :, i * LANES:(i + 1) * LANES].reshape(rows, LANES))

    def y_copy(p):
        return remote(w_oth.at[p], y_got.at[p], y_send.at[p], y_recv.at[p], seq=d_y)

    def a_copy(p):
        return remote(w_alpha.at[p], w_alpha.at[p], a_send.at[p], a_recv.at[p], seq=d_rim)

    def b_copy(p):
        return remote(w_beta.at[p], w_beta.at[p], b_send.at[p], b_recv.at[p], seq=d_rim)

    def o_copy(p):
        return remote(w_alpha.at[p, unit:], o_got.at[p], o_send.at[p], o_recv.at[p], seq=d_y)

    def weights(p):
        pg_wait(1, p)
        pg_wait(2, p)
        grads = jnp.concatenate(
            [pg_s[p].astype(bf16)] + [gat[i, p].astype(bf16) for i in range(3)], axis=0)
        w_oth[p] = dot_f32(tok_t[3 * unit:6 * unit, :], grads)
        y_copy(p).start()
        w_alpha[p] = dot_f32(tok_t[6 * unit:, :], grads)
        a_copy(p).start()
        w_own[p] = dot_f32(tok_t[:3 * unit, :], grads)

    def combine(p):
        y_copy(p).wait_recv()
        w_beta[p] = w_own[p, 2 * unit:] + y_got[p, 2 * unit:]
        b_copy(p).start()
        wg_ref[:, lanes(p)] = w_own[p, :2 * unit] + y_got[p, :2 * unit]

    def pass_on(p):
        a_copy(p).wait_recv()
        o_copy(p).start()

    def close(p):
        o_copy(p).wait_recv()
        b_copy(p).wait_recv()
        wg_ref[:unit, lanes(p)] = w_alpha[p, :unit] + o_got[p]
        wg_ref[unit:, lanes(p)] = w_beta[p]

    first = width // step_cols
    early, follow = WINDOW

    def by_z(values):
        return jnp.where(z < 2, jnp.where(z == 0, values[0], values[1]), jnp.where(z == 2, values[2], values[3]))

    back_begin = by_z(BACK)
    begin = back_begin + RES
    ahead_begin = by_z(AHEAD)
    out_begin = by_z(OUT)
    send_begin = by_z(SEND)
    relay_begin = by_z(RELAY)
    w_first, w_gap, w_rest = WSLOT

    def within(k, low=0, high=pairs):
        return jnp.logical_and(k >= low, k < high)

    def slot_step(s, carry):
        at = pl.when
        spaced = jnp.where(lax.rem(s - w_first + 4 * w_gap * pairs, w_gap) == 0, (s - w_first) // w_gap, -1)
        turn = jnp.where(s < w_rest, spaced, s - w_rest + (w_rest - w_first) // w_gap)

        @at(within(s - min(BACK), 0, pairs // 2))
        def _():
            lane_copy(0, s - min(BACK)).wait_recv()

        @at(within(s - back_begin, 0, pairs // 2))
        def _():
            chain(0, s - back_begin)

        @at(within(s - ahead_begin, 0, pairs // 2))
        def _():
            chain(1, s - ahead_begin)

        for which, when in enumerate(TOKENS):
            for i in range(3):
                if which in (1, 2) and i < 2:
                    continue

                @at(jnp.logical_and(s == when[i], z == which))
                def _():
                    (t_far() if i == 2 else t_near(i, (h, hx)[i])).start()

        @at(s == 0)
        def _():
            prepare()

        @at(s < first)
        def _():
            project(s)

        @at(within(s - LANE, 0, pairs // 2))
        def _():
            lane_copy(1, s - LANE).start()

        @at(within(s - first))
        def _():
            mix(s - first)

        @at(within(s - begin))
        def _():
            gradient(s - begin)

        @at(within(s - send_begin, 0, jnp.where(hub, early, pairs)))
        def _():
            pg_copy(s - send_begin).start()

        relayed = jnp.where(within(s - relay_begin, 0, follow), s - relay_begin, jnp.where(turn >= 0, turn + follow, -1))

        @at(jnp.logical_and(hub, within(relayed)))
        def _():
            pg_wait(0, relayed)
            relay_copy(relayed).start()

        @at(jnp.logical_and(hub, jnp.logical_and(turn >= 0, turn + early < pairs)))
        def _():
            pg_copy(turn + early).start()

        @at(hub)
        def _():
            @at(s == 2)
            def _():
                build_own()

            for which, (near, far, rims) in ((1, TAKE[0]), (2, TAKE[1])):
                for slot, when in ((1, far), (2, rims)):
                    @at(jnp.logical_and(s == when[0], z == which))
                    def _():
                        tk_wait(slot, h)
                        x_copy(slot).start()
                        core_copy(slot, 0).start()

                    @at(jnp.logical_and(s == when[1], z == which))
                    def _():
                        tk_wait(slot, hx)
                        core_copy(slot, 1).start()

                @at(jnp.logical_and(s == near, z == which))
                def _():
                    for i in range(2):
                        tk_wait(0, (h, hx)[i])
                        core_copy(0, i).start()

            for slot in range(3):
                @at(s == BUILD[slot])
                def _():
                    tk_wait(slot, hc)
                    tk_wait(slot, hxc)
                    build_from(slot)

        @at(jnp.logical_and(hub, within(turn)))
        def _():
            weights(turn)

        @at(jnp.logical_and(hub, within(turn - 1)))
        def _():
            combine(turn - 1)

        @at(jnp.logical_and(rim, within(turn - 1)))
        def _():
            pass_on(turn - 1)

        @at(jnp.logical_and(rim, within(turn - 2)))
        def _():
            close(turn - 2)

        @at(within(s - out_begin))
        def _():
            output(s - out_begin)

        for o in range(nh):
            @at(s == by_z(TG) + (o - 1) % nh)
            def _():
                input_part(o)

        @at(s == out_begin + pairs)
        def _():
            strict_ones = (row_ids > col_ids).astype(f32)
            which = lax.broadcasted_iota(jnp.int32, (heads, pairs), 0) // per
            row = (which == lax.broadcasted_iota(jnp.int32, (heads, pairs), 1)).astype(f32)
            mine = (lax.rem(lax.broadcasted_iota(jnp.int32, (heads, LANES), 0), per)
                    == lax.broadcasted_iota(jnp.int32, (heads, LANES), 1) // hdim)
            through = jnp.sum(jnp.where(mine, dot_exact(row, th_s[...]), 0.0), axis=1, keepdims=True)
            dg_ref[...] = (dot_exact(q1_s[...], lower_ones, ROWS)
                           + dot_exact(q2_s[...], strict_ones, (((0,), (1,)), ((), ()))) + through)

        @at(s == total_slots - 3)
        def _():
            total = part[0]
            for o in range(1, nh):
                g_copy(o).wait()
                total = total + got[o]
            tg_ref[...] = jnp.transpose(total).astype(bf16)

        return carry

    total_slots = w_rest + pairs + 2 - (w_rest - w_first) // w_gap
    lax.fori_loop(0, total_slots, slot_step, 0)

    t_far().wait_send()

    @pl.when(hub)
    def _():
        for slot in range(3):
            for i in range(2):
                core_copy(slot, i).wait_send()
            if slot:
                x_copy(slot).wait_send()

    @pl.when(rim)
    def _():
        t_near(0, h).wait_send()
        t_near(1, hx).wait_send()

    def drain(k, carry):
        @pl.when(k < pairs // 2)
        def _():
            for kind in range(2):
                lane_copy(kind, k).wait_send()
                result_copy(kind, k, 2 * k + y).wait_send()

                @pl.when(z != (0, n // 2 - 1)[kind])
                def _():
                    next_copy(kind, k).wait_send()

        pg_copy(k).wait_send()

        @pl.when(hub)
        def _():
            relay_copy(k).wait_send()
            y_copy(k).wait_send()
            a_copy(k).wait_send()
            b_copy(k).wait_send()

        @pl.when(rim)
        def _():
            o_copy(k).wait_send()

        return carry

    lax.fori_loop(0, pairs, drain, 0)


def hub_call(*args):
    n, nh = lax.axis_size("seq"), lax.axis_size("head")
    tokens, x_weight, b_input, _, log_decay, _, cotangent = args
    rows, width = cotangent.shape
    depth = tokens.shape[1]
    heads, state = log_decay.shape[0], b_input.shape[1]
    pairs = width // LANES
    half, unit, quarter, tcols = depth // 2, depth // (2 * n), rows // nh, depth // nh
    vm = pl.BlockSpec(memory_space=pltpu.VMEM)
    anywhere = pl.BlockSpec(memory_space=pl.ANY)
    dma = pltpu.SemaphoreType.DMA
    wide = pltpu.VMEM((pairs, rows, LANES), f32)

    def states(more=0, split=1):
        return pltpu.VMEM((pairs // split, state + more, LANES), f32)

    def blocks(count):
        return pltpu.VMEM((pairs, count * unit, LANES), f32)

    scratch = [
        pltpu.VMEM((pairs, rows, LANES), bf16), wide, wide, wide, pltpu.VMEM((heads, rows), f32),
        wide, wide, wide, pltpu.VMEM((rows, rows), f32), states(), states(8), states(0, 2), states(8, 2),
        states(0, 2), states(0, 2), states(0, 2), states(0, 2), states(0, 2), states(0, 2), states(), states(),
        pltpu.VMEM((rows, heads), f32), pltpu.VMEM((rows, heads), f32), pltpu.VMEM((pairs, LANES), f32),
        pltpu.VMEM(x_weight.shape, bf16), pltpu.VMEM(tokens.shape, bf16), pltpu.VMEM(cotangent.shape, bf16),
        wide, pltpu.VMEM((width, rows), bf16),
        pltpu.VMEM((3, pairs, rows, LANES), f32), pltpu.VMEM((3, quarter, half), f32),
        pltpu.VMEM((3, nh, quarter, half), f32), pltpu.VMEM((half, 4 * rows), bf16),
        blocks(3), blocks(3), blocks(2), blocks(1), blocks(3), blocks(1),
        pltpu.VMEM((nh, tcols, rows), f32), pltpu.VMEM((nh, tcols, rows), f32),
        dma((3,)), dma((2, 3, pairs // 2)), dma((2, 3, pairs // 2)),
        dma((pairs,)), dma((3, pairs)), dma((pairs,)), dma((3,)), dma((3, nh)), dma((3, 2)), dma((3,)),
        dma((pairs,)), dma((pairs,)), dma((pairs,)), dma((pairs,)), dma((pairs,)), dma((pairs,)),
        dma((pairs,)), dma((pairs,)), dma((nh,)), dma((nh,))]
    outs = [jax.ShapeDtypeStruct((rows, width), bf16), jax.ShapeDtypeStruct((heads, rows), f32),
            jax.ShapeDtypeStruct((depth // n, width), f32), jax.ShapeDtypeStruct((rows, tcols), bf16)]
    return pl.pallas_call(
        functools.partial(hub_kernel, n, nh),
        out_shape=outs,
        in_specs=[anywhere] * 2 + [vm] * 4 + [anywhere],
        out_specs=[vm] * len(outs),
        scratch_shapes=scratch,
        compiler_params=pltpu.CompilerParams(
            collective_id=1, has_side_effects=True, vmem_limit_bytes=60 << 20),
        cost_estimate=pl.CostEstimate(
            flops=6 * rows * depth * width, bytes_accessed=12 << 20, transcendentals=1 << 20),
        name="hub",
    )(*args)


def hand_kernel(count, *refs):
    ins, outs, mids = refs[:count], refs[count:2 * count], refs[2 * count:3 * count]
    sems = refs[3 * count]
    first = [pltpu.make_async_copy(a, m, sems.at[0, i]) for i, (a, m) in enumerate(zip(ins, mids))]
    second = [pltpu.make_async_copy(m, b, sems.at[1, i]) for i, (m, b) in enumerate(zip(mids, outs))]
    for copy in first:
        copy.start()
    for one, two in zip(first, second):
        one.wait()
        two.start()
    for copy in second:
        copy.wait()


def hand_over(*arrays):
    anywhere = pl.BlockSpec(memory_space=pl.ANY)
    count = len(arrays)
    return pl.pallas_call(
        functools.partial(hand_kernel, count),
        out_shape=[jax.ShapeDtypeStruct(a.shape, a.dtype) for a in arrays],
        in_specs=[anywhere] * count,
        out_specs=[anywhere] * count,
        scratch_shapes=[pltpu.VMEM(a.shape, a.dtype) for a in arrays]
        + [pltpu.SemaphoreType.DMA((2, count))],
        name="hand_over",
    )(*arrays)


def per_device(tokens, x_weight, b_input, c_input, log_decay, step_size, cotangent):
    n, nh = lax.axis_size("seq"), lax.axis_size("head")
    rows, depth = tokens.shape
    assert rows == SPAN and n % 2 == 0
    args = (tokens, x_weight, b_input, c_input, log_decay.T, step_size.T, cotangent)
    if n == 8 and nh == 4:
        y, dg, wg, tg = hub_call(*args)
        y, wg, tg = hand_over(y, wg, tg)
        return y, tg, wg, dg.T
    y, pg, dg = span_call(n, *args)
    pgb = pg.astype(bf16)
    wg = lax.psum_scatter(dot_f32(tokens, pgb, ROWS), "seq", scatter_dimension=0, tiled=True)
    tg = lax.psum_scatter(dot_f32(pgb, x_weight, COLS), "head", scatter_dimension=1, tiled=True)
    return y, tg.astype(bf16), wg, dg.T


def solution(mesh):
    return jax.shard_map(
        per_device,
        mesh=mesh,
        in_specs=(
            P("seq", None),
            P(None, "head"),
            P("seq", None),
            P("seq", None),
            P("seq", "head"),
            P("seq", "head"),
            P("seq", "head"),
        ),
        out_specs=(P("seq", "head"), P("seq", "head"), P("seq", "head"), P("seq", "head")),
        check_vma=False,
    )
```

```python
import functools
import math

import jax
import jax.numpy as jnp
from jax import lax
from jax.experimental import pallas as pl
from jax.experimental.pallas import tpu as pltpu
from jax.sharding import PartitionSpec as P

SPAN = 256
LANES = 128
MESH = pl.DeviceIdType.MESH
highest = lax.Precision.HIGHEST
f32 = jnp.float32
bf16 = jnp.bfloat16


def dot_f32(a, b, dims=(((1,), (0,)), ((), ()))):
    return lax.dot_general(a, b, dims, preferred_element_type=f32)


def dot_exact(a, b, dims=(((1,), (0,)), ((), ()))):
    return lax.dot_general(a, b, dims, preferred_element_type=f32, precision=highest)


ROWS = (((0,), (0,)), ((), ()))
COLS = (((1,), (1,)), ((), ()))


def split_two(a):
    high = a.astype(bf16)
    return high, (a - high.astype(f32)).astype(bf16)


def span_kernel(n, *refs):
    tok, xw_hbm, b_ref, c_ref, ld, st, cot, y_ref, pg_ref, dg_ref = refs[:10]
    (x_s, pre_s, ce_s, st_s, cum_t, inner_s, back_s, score_s, loc_f, loc_b, out_f, out_b,
     prior, adj, q1_s, q2_s, th_s, xw, xw_sem, send_f, recv_f, send_b, recv_b) = refs[10:]
    d = lax.axis_index("seq")
    rows, width = cot.shape
    heads = ld.shape[0]
    hdim = width // heads
    pairs = width // LANES
    per = LANES // hdim
    load = pltpu.make_async_copy(xw_hbm, xw, xw_sem)
    load.start()

    barrier = pltpu.get_barrier_semaphore()
    for o in (1, n - 1):
        pl.semaphore_signal(barrier, 1, device_id={"seq": lax.rem(d + o, n)}, device_id_type=MESH)
    pl.semaphore_wait(barrier, 2)

    row_ids = lax.broadcasted_iota(jnp.int32, (rows, rows), 0)
    col_ids = lax.broadcasted_iota(jnp.int32, (rows, rows), 1)
    lower = row_ids >= col_ids
    lower_ones = lower.astype(f32)
    decay = ld[...]
    cum = dot_exact(lower_ones, decay, COLS)
    cum_t[...] = dot_exact(decay, lower_ones, COLS)
    spread = (lax.broadcasted_iota(jnp.int32, (heads, width), 0)
              == lax.broadcasted_iota(jnp.int32, (heads, width), 1) // hdim).astype(f32)
    wide_cum = dot_exact(cum, spread)
    wide_step = dot_exact(st[...], spread, ROWS)
    for p in range(pairs):
        ce_s[p] = wide_cum[:, p * LANES:(p + 1) * LANES]
        st_s[p] = wide_step[:, p * LANES:(p + 1) * LANES]
    b_val, c_val = b_ref[...], c_ref[...]
    score_s[...] = jnp.where(lower, dot_f32(c_val, b_val, COLS), 0.0)
    q1_s[...] = jnp.zeros_like(q1_s)
    q2_s[...] = jnp.zeros_like(q2_s)
    th_s[...] = jnp.zeros_like(th_s)

    load.wait()
    step_cols = 2 * LANES
    for k in range(width // step_cols):
        cols = slice(k * step_cols, (k + 1) * step_cols)
        ce = wide_cum[:, cols]
        gw = (cot[:, cols].astype(f32) * jnp.exp(ce)).astype(bf16)
        grad_k = dot_f32(c_val, gw, ROWS)
        pre = dot_f32(tok[...], xw[:, cols])
        act = pre / (1.0 + jnp.exp(-pre))
        xk = (act * wide_step[:, cols]).astype(bf16)
        xwk = (xk.astype(f32) * jnp.exp(ce[rows - 1:rows] - ce)).astype(bf16)
        state_k = dot_f32(b_val, xwk, ROWS)
        for i in range(2):
            at = slice(i * LANES, (i + 1) * LANES)
            pre_s[2 * k + i] = pre[:, at]
            x_s[2 * k + i] = xk[:, at]
            loc_b[2 * k + i] = grad_k[:, at]
            loc_f[2 * k + i] = state_k[:, at]

    @pl.when(d == 0)
    def _():
        prior[...] = jnp.zeros_like(prior)

    @pl.when(d == n - 1)
    def _():
        adj[...] = jnp.zeros_like(adj)

    def fcopy(k):
        return pltpu.make_async_remote_copy(
            src_ref=out_f.at[k], dst_ref=prior.at[k], send_sem=send_f.at[k], recv_sem=recv_f.at[k],
            device_id={"seq": lax.rem(d + 1, n)}, device_id_type=MESH)

    def bcopy(k):
        return pltpu.make_async_remote_copy(
            src_ref=out_b.at[k], dst_ref=adj.at[k], send_sem=send_b.at[k], recv_sem=recv_b.at[k],
            device_id={"seq": lax.rem(d + n - 1, n)}, device_id_type=MESH)

    lane = lax.broadcasted_iota(jnp.int32, (rows, LANES), 1)

    def mix(p):
        ce = ce_s[p]
        xp = x_s[p]
        gp = cot[:, pl.ds(pl.multiple_of(p * LANES, LANES), LANES)]
        inner = back = None
        for i in range(per):
            gap = ce[:, i * hdim:i * hdim + 1] - cum_t[pl.ds(per * p + i, 1), :]
            m = (score_s[...] * jnp.exp(jnp.minimum(gap, 0.0))).astype(bf16)
            inner_i = dot_f32(m, xp)
            back_i = dot_f32(m, gp, ROWS)
            if inner is None:
                inner, back = inner_i, back_i
            else:
                inner = jnp.where(lane < i * hdim, inner, inner_i)
                back = jnp.where(lane < i * hdim, back, back_i)
        inner_s[p] = inner
        back_s[p] = back

    def finish(p):
        ce = ce_s[p]
        end = ce[rows - 1:rows]
        at = pl.ds(pl.multiple_of(p * LANES, LANES), LANES)
        pr, ad = prior[p], adj[p]
        hi, lo = split_two(ad)
        bc = jnp.exp(end - ce) * (dot_f32(b_val, hi) + dot_f32(b_val, lo))
        bi = back_s[p]
        pre = pre_s[p]
        sig = 1.0 / (1.0 + jnp.exp(-pre))
        pg = (bi + bc) * st_s[p] * sig * (1.0 + pre * (1.0 - sig))
        pg_ref[:, at] = pg.astype(bf16).astype(f32)
        grad = cot[:, at].astype(f32)
        x = x_s[p].astype(f32)
        hi, lo = split_two(pr)
        y = inner_s[p] + jnp.exp(ce) * (dot_f32(c_val, hi) + dot_f32(c_val, lo))
        y_ref[:, at] = y.astype(bf16)
        pick = (lax.broadcasted_iota(jnp.int32, (LANES, heads), 0) // hdim + per * p
                == lax.broadcasted_iota(jnp.int32, (LANES, heads), 1)).astype(f32)
        q1_s[...] += dot_exact(grad * y - x * bi, pick)
        q2_s[...] += dot_exact(x * bc, pick)
        through = jnp.exp(end) * jnp.sum(pr * ad, axis=0, keepdims=True)
        th_s[...] += dot_exact(pick, jnp.broadcast_to(through, (8, LANES)), (((0,), (1,)), ((), ())))

    def chain(s, carry):
        kf = s - d

        @pl.when(jnp.logical_and(kf >= 0, kf < pairs))
        def _():
            @pl.when(d > 0)
            def _():
                fcopy(kf).wait_recv()

            @pl.when(d < n - 1)
            def _():
                out_f[kf] = jnp.exp(ce_s[kf, rows - 1:rows, :]) * prior[kf] + loc_f[kf]
                fcopy(kf).start()

        kb = s - (n - 1 - d)

        @pl.when(jnp.logical_and(kb >= 0, kb < pairs))
        def _():
            @pl.when(d < n - 1)
            def _():
                bcopy(kb).wait_recv()

            @pl.when(d > 0)
            def _():
                out_b[kb] = jnp.exp(ce_s[kb, rows - 1:rows, :]) * adj[kb] + loc_b[kb]
                bcopy(kb).start()

        @pl.when(s < pairs)
        def _():
            mix(s)

        ks = s - (n - 1)

        @pl.when(jnp.logical_and(ks >= 0, ks < pairs))
        def _():
            finish(ks)

        return carry

    lax.fori_loop(0, n - 1 + pairs, chain, 0)

    strict_ones = (row_ids > col_ids).astype(f32)
    dg_ref[...] = (dot_exact(q1_s[...], lower_ones, ROWS)
                   + dot_exact(q2_s[...], strict_ones, (((0,), (1,)), ((), ()))) + th_s[:, 0:1])

    @pl.when(d < n - 1)
    def _():
        def one(k, carry):
            fcopy(k).wait_send()
            return carry
        lax.fori_loop(0, pairs, one, 0)

    @pl.when(d > 0)
    def _():
        def one(k, carry):
            bcopy(k).wait_send()
            return carry
        lax.fori_loop(0, pairs, one, 0)


def span_call(n, *args):
    _, x_weight, b_input, _, log_decay, _, cotangent = args
    depth = x_weight.shape[0]
    rows, width = cotangent.shape
    heads, state = log_decay.shape[0], b_input.shape[1]
    pairs = width // LANES
    vm = pl.BlockSpec(memory_space=pltpu.VMEM)
    wide = pltpu.VMEM((pairs, rows, LANES), f32)
    states = pltpu.VMEM((pairs, state, LANES), f32)
    dma = pltpu.SemaphoreType.DMA
    scratch = [
        pltpu.VMEM((pairs, rows, LANES), bf16), wide, wide, wide, pltpu.VMEM((heads, rows), f32),
        wide, wide, pltpu.VMEM((rows, rows), f32), states, states, states, states, states, states,
        pltpu.VMEM((rows, heads), f32), pltpu.VMEM((rows, heads), f32), pltpu.VMEM((heads, 8), f32),
        pltpu.VMEM(x_weight.shape, bf16), dma(()), dma((pairs,)), dma((pairs,)), dma((pairs,)), dma((pairs,))]
    outs = [jax.ShapeDtypeStruct((rows, width), bf16), jax.ShapeDtypeStruct((rows, width), f32),
            jax.ShapeDtypeStruct((heads, rows), f32)]
    return pl.pallas_call(
        functools.partial(span_kernel, n),
        out_shape=outs,
        in_specs=[vm, pl.BlockSpec(memory_space=pl.ANY)] + [vm] * (len(args) - 2),
        out_specs=[vm] * len(outs),
        scratch_shapes=scratch,
        compiler_params=pltpu.CompilerParams(
            collective_id=0, has_side_effects=True, vmem_limit_bytes=60 << 20),
        cost_estimate=pl.CostEstimate(
            flops=6 * rows * depth * width, bytes_accessed=12 << 20, transcendentals=1 << 20),
        name="span",
    )(*args)


WINDOW = (3, 2)
RES = 3
BACK = (11, 8, 5, 2)
AHEAD = (9, 12, 15, 18)
OUT = (14, 24, 24, 23)
SEND = (14, 11, 12, 8)
RELAY = (0, 17, 12, 0)
LANE = 3
TG = (24, 25, 25, 18)
TOKENS = ((0, 1, 0), (0, 0, 0), (0, 0, 0), (10, 10, 6))
TAKE = ((17, (8, 12), (16, 19)), (19, (11, 15), (13, 17)))
BUILD = (20, 18, 21)
WSLOT = (21, 2, 25)


def hub_kernel(n, nh, *refs):
    tok_hbm, xw_hbm, b_ref, c_ref, ld, st, cot_hbm, y_ref, dg_ref, wg_ref, tg_ref = refs[:11]
    (x_s, pre_s, ce_s, st_s, cum_t, inner_s, back_s, bc_s, score_s, loc_f, loc_b, got_f, got_b, in_f, in_b, out_f, out_b,
     res_f, res_b, prior, adj,
     q1_s, q2_s, th_s, xw, tok, cot, pg_s, pg_t, gat, tsend, tk, tok_t, w_own, w_oth, w_alpha, w_beta, y_got, o_got,
     part, got, xw_sem, ch_send, ch_recv, pg_send, pg_recv, rl_send, t_send, tk_recv, tf_send,
     tx_send, y_send, y_recv, a_send, a_recv, b_send, b_recv, o_send, o_recv, g_send, g_recv) = refs[11:]
    d, h = lax.axis_index("seq"), lax.axis_index("head")
    rows, width = cot.shape
    depth = tok.shape[1]
    heads = ld.shape[0]
    hdim = width // heads
    pairs = width // LANES
    per = LANES // hdim
    quarter, half = rows // nh, depth // 2
    unit = depth // (2 * n)
    state = b_ref.shape[1]
    z, y = d // 2, lax.rem(d, 2)
    side = z // 2
    hub = jnp.logical_or(z == 1, z == 2)
    rim = jnp.logical_not(hub)
    d_near = (1 + side) * 2 + y
    d_far = (2 - side) * 2 + y
    d_rim = 3 * side * 2 + y
    d_y = d + 1 - 2 * y
    hx = lax.rem(h + 2, nh)
    hc = h + 1 - 2 * lax.rem(h, 2)
    hxc = lax.rem(hc + 2, nh)
    load_cot = pltpu.make_async_copy(cot_hbm, cot, xw_sem.at[0])
    load_tok = pltpu.make_async_copy(tok_hbm, tok, xw_sem.at[1])
    load = pltpu.make_async_copy(xw_hbm, xw, xw_sem.at[2])
    for copy in (load_cot, load_tok, load):
        copy.start()

    def remote(src, dst, send, recv, **to):
        return pltpu.make_async_remote_copy(
            src_ref=src, dst_ref=dst, send_sem=send, recv_sem=recv, device_id=to, device_id_type=MESH)

    barrier = pltpu.get_barrier_semaphore()
    for o in range(1, n):
        pl.semaphore_signal(barrier, 1, device_id={"seq": lax.rem(d + o, n)}, device_id_type=MESH)
    for o in range(1, nh):
        pl.semaphore_signal(barrier, 1, device_id={"head": lax.rem(h + o, nh)}, device_id_type=MESH)

    def token_rows(q, which):
        return tok[pl.ds(pl.multiple_of(q * quarter, quarter), quarter),
                   pl.ds(pl.multiple_of(which * half, half), half)].astype(f32)

    def t_far():
        slot = jnp.where(rim, 2, 1)
        return remote(tsend.at[2], tk.at[slot, h], t_send.at[2], tk_recv.at[slot, h], seq=d_far)

    def t_near(i, q):
        return remote(tsend.at[i], tk.at[0, q], t_send.at[i], tk_recv.at[0, q], seq=d_near)

    row_ids = lax.broadcasted_iota(jnp.int32, (rows, rows), 0)
    col_ids = lax.broadcasted_iota(jnp.int32, (rows, rows), 1)
    lower = row_ids >= col_ids
    lower_ones = lower.astype(f32)
    decay = ld[...]
    cum = dot_exact(lower_ones, decay, COLS)
    spread = (lax.broadcasted_iota(jnp.int32, (heads, width), 0)
              == lax.broadcasted_iota(jnp.int32, (heads, width), 1) // hdim).astype(f32)
    wide_cum = dot_exact(cum, spread)
    step_cols = 2 * LANES
    load_cot.wait()
    for k in range(width // step_cols):
        cols = slice(k * step_cols, (k + 1) * step_cols)
        ce = wide_cum[:, cols]
        gw = (cot[:, cols].astype(f32) * jnp.exp(ce)).astype(bf16)
        grad_k = dot_f32(c_ref[...], gw, ROWS)
        for i in range(2):
            at = slice(i * LANES, (i + 1) * LANES)
            ce_s[2 * k + i] = ce[:, at]
            loc_b[2 * k + i, :state] = grad_k[:, at]
            loc_b[2 * k + i, state:] = jnp.broadcast_to(jnp.exp(ce[rows - 1:rows, at]), (8, LANES))

    @pl.when(z == 0)
    def _():
        in_f[...] = jnp.zeros_like(in_f)

    @pl.when(z == n // 2 - 1)
    def _():
        in_b[...] = jnp.zeros_like(in_b)

    def lane_copy(kind, j):
        src, dst = ((loc_b, got_b), (loc_f, got_f))[kind]
        return remote(src.at[2 * j + 1 - y], dst.at[j], ch_send.at[kind, 0, j], ch_recv.at[kind, 0, j], seq=d_y)

    def next_copy(kind, j):
        src, dst = ((out_b, in_b), (out_f, in_f))[kind]
        to = lax.rem(d + (2 if kind else n - 2), n)
        return remote(src.at[j], dst.at[j], ch_send.at[kind, 1, j], ch_recv.at[kind, 1, j], seq=to)

    def result_copy(kind, j, p):
        src, dst = ((res_b, adj), (res_f, prior))[kind]
        return remote(src.at[j], dst.at[p], ch_send.at[kind, 2, j], ch_recv.at[kind, 2, j], seq=d_y)

    def chain(kind, j):
        p = 2 * j + y
        if kind:
            lane_copy(kind, j).wait_recv()
        begins, ends = (n // 2 - 1, 0) if kind == 0 else (0, n // 2 - 1)

        @pl.when(z != begins)
        def _():
            next_copy(kind, j).wait_recv()

        arrives = (in_b, in_f)[kind][j]
        mine, other = (loc_b[p, :state], got_b[j, :state]) if kind == 0 else (loc_f[p], got_f[j])
        my_end, other_end = loc_b[p, state:state + 1], got_b[j, state:state + 1]
        head = y == 1 - kind
        one = jnp.where(head, mine, other) + jnp.where(head, my_end, other_end) * arrives
        two = jnp.where(head, other, mine) + jnp.where(head, other_end, my_end) * one

        @pl.when(z != ends)
        def _():
            (out_b, out_f)[kind][j] = two
            next_copy(kind, j).start()

        (res_b, res_f)[kind][j] = jnp.where(head, one, arrives)
        result_copy(kind, j, p).start()
        (adj, prior)[kind][p] = jnp.where(head, arrives, one)

    def chain_result(kind, p):
        @pl.when(lax.rem(p, 2) != y)
        def _():
            result_copy(kind, p // 2, p).wait_recv()

    load_tok.wait()
    tsend[2] = token_rows(h, 1 - side)

    @pl.when(rim)
    def _():
        tsend[0] = token_rows(h, side)
        tsend[1] = token_rows(hx, side)
    pl.semaphore_wait(barrier, n + nh - 2)
    for j in range(pairs // 2):
        lane_copy(0, j).start()

    def prepare():
        cum_t[...] = dot_exact(decay, lower_ones, COLS)
        wide_step = dot_exact(st[...], spread, ROWS)
        for p in range(pairs):
            st_s[p] = wide_step[:, p * LANES:(p + 1) * LANES]
        score_s[...] = jnp.where(lower, dot_f32(c_ref[...], b_ref[...], COLS), 0.0)
        q1_s[...] = jnp.zeros_like(q1_s)
        q2_s[...] = jnp.zeros_like(q2_s)
        th_s[...] = jnp.zeros_like(th_s)
        load.wait()

    def project(k):
        pre = dot_f32(tok[...], xw[:, pl.ds(pl.multiple_of(k * step_cols, step_cols), step_cols)])
        for i in range(2):
            p = 2 * k + i
            pre_i = pre[:, i * LANES:(i + 1) * LANES]
            ce = ce_s[p]
            act = pre_i / (1.0 + jnp.exp(-pre_i))
            xk = (act * st_s[p]).astype(bf16)
            xwk = (xk.astype(f32) * jnp.exp(ce[rows - 1:rows] - ce)).astype(bf16)
            pre_s[p] = pre_i
            x_s[p] = xk
            loc_f[p] = dot_f32(b_ref[...], xwk, ROWS)

    lane = lax.broadcasted_iota(jnp.int32, (rows, LANES), 1)

    def lanes(p):
        return pl.ds(pl.multiple_of(p * LANES, LANES), LANES)

    def mix(p):
        ce = ce_s[p]
        xp = x_s[p]
        gp = cot[:, lanes(p)]
        inner = back = None
        for i in range(per):
            gap = ce[:, i * hdim:i * hdim + 1] - cum_t[pl.ds(per * p + i, 1), :]
            m = (score_s[...] * jnp.exp(jnp.minimum(gap, 0.0))).astype(bf16)
            inner_i = dot_f32(m, xp)
            back_i = dot_f32(m, gp, ROWS)
            if inner is None:
                inner, back = inner_i, back_i
            else:
                inner = jnp.where(lane < i * hdim, inner, inner_i)
                back = jnp.where(lane < i * hdim, back, back_i)
        inner_s[p] = inner
        back_s[p] = back

    def pg_copy(p):
        slot = jnp.where(rim, 0, 1)
        return remote(pg_s.at[p], gat.at[slot, p], pg_send.at[p], pg_recv.at[slot, p],
                      seq=jnp.where(rim, d_near, d_far))

    def relay_copy(p):
        return remote(gat.at[0, p], gat.at[2, p], rl_send.at[p], pg_recv.at[2, p], seq=d_far)

    def pg_wait(slot, p):
        remote(pg_s.at[p], gat.at[slot, p], pg_send.at[p], pg_recv.at[slot, p], seq=d_far).wait_recv()

    def gradient(p):
        ce = ce_s[p]
        chain_result(0, p)
        hi, lo = split_two(adj[p])
        bc = jnp.exp(ce[rows - 1:rows] - ce) * (dot_f32(b_ref[...], hi) + dot_f32(b_ref[...], lo))
        bc_s[p] = bc
        pre = pre_s[p]
        sig = 1.0 / (1.0 + jnp.exp(-pre))
        pg = (back_s[p] + bc) * st_s[p] * sig * (1.0 + pre * (1.0 - sig))
        pg = pg.astype(bf16).astype(f32)
        pg_s[p] = pg
        pg_t[lanes(p), :] = jnp.transpose(pg).astype(bf16)

    def by_head(value, p):
        pick = (lax.rem(lax.broadcasted_iota(jnp.int32, (2 * LANES, heads), 0), LANES) // hdim + per * p
                == lax.broadcasted_iota(jnp.int32, (2 * LANES, heads), 1)).astype(bf16)
        return dot_f32(jnp.concatenate(split_two(value), axis=1), pick)

    def output(p):
        chain_result(1, p)
        ce = ce_s[p]
        pr, ad = prior[p], adj[p]
        grad = cot[:, lanes(p)].astype(f32)
        x = x_s[p].astype(f32)
        hi, lo = split_two(pr)
        out = inner_s[p] + jnp.exp(ce) * (dot_f32(c_ref[...], hi) + dot_f32(c_ref[...], lo))
        y_ref[:, lanes(p)] = out.astype(bf16)
        q1_s[...] += by_head(grad * out - x * back_s[p], p)
        q2_s[...] += by_head(x * bc_s[p], p)
        th_s[pl.ds(p, 1), :] = jnp.exp(ce[rows - 1:rows]) * jnp.sum(pr * ad, axis=0, keepdims=True)

    def g_copy(o):
        return remote(part.at[o], got.at[o], g_send.at[o], g_recv.at[o], head=lax.rem(h + o, nh))

    def input_part(o):
        tcols = part.shape[1]
        to = lax.rem(h + o, nh)
        part[o] = dot_f32(xw[pl.ds(pl.multiple_of(to * tcols, tcols), tcols), :], pg_t[...])
        if o:
            g_copy(o).start()

    def tk_wait(slot, q):
        remote(tk.at[slot, q], tk.at[slot, q], t_send.at[0], tk_recv.at[slot, q], seq=d_y).wait_recv()

    def core_copy(slot, i):
        q = (h, hx)[i]
        return remote(tk.at[slot, q], tk.at[slot, q], tf_send.at[slot, i], tk_recv.at[slot, q], head=hc)

    def x_copy(slot):
        return remote(tk.at[slot, h], tk.at[slot, h], tx_send.at[slot], tk_recv.at[slot, h], head=hx)

    at_row = []
    for i in range(n // 2):
        for a in range(2):
            own = y == i % 2
            on_hub = jnp.where(own, 0, 3 * unit) + a * unit
            on_rim = jnp.where(own, 2, 5) * unit if a else jnp.where(own, 6, 7) * unit
            at_row.append(jnp.where(side == 1 - i // 2, on_hub, on_rim))
    piece = math.gcd(LANES, unit)

    def build(block, source):
        for i in range(half // LANES):
            turned = jnp.transpose(source(i)).astype(bf16)
            for j in range(LANES // piece):
                r = i * LANES + j * piece
                tok_t[pl.ds(pl.multiple_of(at_row[r // unit] + r % unit, piece), piece),
                      block * rows:(block + 1) * rows] = turned[j * piece:(j + 1) * piece]

    def build_own():
        build(0, lambda i: tok[:, pl.ds(pl.multiple_of(side * half + i * LANES, LANES), LANES)].astype(f32))

    def build_from(slot):
        build(slot + 1, lambda i: tk[slot, :, :, i * LANES:(i + 1) * LANES].reshape(rows, LANES))

    def y_copy(p):
        return remote(w_oth.at[p, :2 * unit], y_got.at[p, :2 * unit], y_send.at[0, p], y_recv.at[0, p], seq=d_y)

    def rim_copy(p):
        return remote(w_oth.at[p, 2 * unit:], y_got.at[p, 2 * unit:], y_send.at[1, p], y_recv.at[1, p], seq=d_y)

    def a_copy(p):
        return remote(w_alpha.at[p], w_alpha.at[p], a_send.at[p], a_recv.at[p], seq=d_rim)

    def b_copy(p):
        return remote(w_beta.at[p], w_beta.at[p], b_send.at[p], b_recv.at[p], seq=d_rim)

    def o_copy(p):
        return remote(w_alpha.at[p, unit:], o_got.at[p], o_send.at[p], o_recv.at[p], seq=d_y)

    def weights(p):
        pg_wait(1, p)
        pg_wait(2, p)
        grads = jnp.concatenate(
            [pg_s[p].astype(bf16)] + [gat[i, p].astype(bf16) for i in range(3)], axis=0)
        w_oth[p] = dot_f32(tok_t[3 * unit:6 * unit, :], grads)
        rim_copy(p).start()
        y_copy(p).start()
        w_alpha[p] = dot_f32(tok_t[6 * unit:, :], grads)
        a_copy(p).start()
        w_own[p] = dot_f32(tok_t[:3 * unit, :], grads)

    def combine(p):
        rim_copy(p).wait_recv()
        w_beta[p] = w_own[p, 2 * unit:] + y_got[p, 2 * unit:]
        b_copy(p).start()
        y_copy(p).wait_recv()
        wg_ref[:, lanes(p)] = w_own[p, :2 * unit] + y_got[p, :2 * unit]

    def pass_on(p):
        a_copy(p).wait_recv()
        o_copy(p).start()

    def close(p):
        o_copy(p).wait_recv()
        b_copy(p).wait_recv()
        wg_ref[:unit, lanes(p)] = w_alpha[p, :unit] + o_got[p]
        wg_ref[unit:, lanes(p)] = w_beta[p]

    first = width // step_cols
    early, follow = WINDOW

    def by_z(values):
        return jnp.where(z < 2, jnp.where(z == 0, values[0], values[1]), jnp.where(z == 2, values[2], values[3]))

    back_begin = by_z(BACK)
    begin = back_begin + RES
    ahead_begin = by_z(AHEAD)
    out_begin = by_z(OUT)
    send_begin = by_z(SEND)
    relay_begin = by_z(RELAY)
    w_first, w_gap, w_rest = WSLOT

    def within(k, low=0, high=pairs):
        return jnp.logical_and(k >= low, k < high)

    def slot_step(s, carry):
        at = pl.when
        spaced = jnp.where(lax.rem(s - w_first + 4 * w_gap * pairs, w_gap) == 0, (s - w_first) // w_gap, -1)
        turn = jnp.where(s < w_rest, spaced, s - w_rest + (w_rest - w_first) // w_gap)

        @at(within(s - min(BACK), 0, pairs // 2))
        def _():
            lane_copy(0, s - min(BACK)).wait_recv()

        @at(within(s - back_begin, 0, pairs // 2))
        def _():
            chain(0, s - back_begin)

        @at(within(s - ahead_begin, 0, pairs // 2))
        def _():
            chain(1, s - ahead_begin)

        for which, when in enumerate(TOKENS):
            for i in range(3):
                if which in (1, 2) and i < 2:
                    continue

                @at(jnp.logical_and(s == when[i], z == which))
                def _():
                    (t_far() if i == 2 else t_near(i, (h, hx)[i])).start()

        @at(s == 0)
        def _():
            prepare()

        @at(s < first)
        def _():
            project(s)

        @at(within(s - LANE, 0, pairs // 2))
        def _():
            lane_copy(1, s - LANE).start()

        @at(within(s - first))
        def _():
            mix(s - first)

        @at(within(s - begin))
        def _():
            gradient(s - begin)

        @at(within(s - send_begin, 0, jnp.where(hub, early, pairs)))
        def _():
            pg_copy(s - send_begin).start()

        relayed = jnp.where(within(s - relay_begin, 0, follow), s - relay_begin, jnp.where(turn >= 0, turn + follow, -1))

        @at(jnp.logical_and(hub, within(relayed)))
        def _():
            pg_wait(0, relayed)
            relay_copy(relayed).start()

        @at(jnp.logical_and(hub, jnp.logical_and(turn >= 0, turn + early < pairs)))
        def _():
            pg_copy(turn + early).start()

        @at(hub)
        def _():
            @at(s == 2)
            def _():
                build_own()

            for which, (near, far, rims) in ((1, TAKE[0]), (2, TAKE[1])):
                for slot, when in ((1, far), (2, rims)):
                    @at(jnp.logical_and(s == when[0], z == which))
                    def _():
                        tk_wait(slot, h)
                        x_copy(slot).start()
                        core_copy(slot, 0).start()

                    @at(jnp.logical_and(s == when[1], z == which))
                    def _():
                        tk_wait(slot, hx)
                        core_copy(slot, 1).start()

                @at(jnp.logical_and(s == near, z == which))
                def _():
                    for i in range(2):
                        tk_wait(0, (h, hx)[i])
                        core_copy(0, i).start()

            for slot in range(3):
                @at(s == BUILD[slot])
                def _():
                    tk_wait(slot, hc)
                    tk_wait(slot, hxc)
                    build_from(slot)

        @at(jnp.logical_and(hub, within(turn)))
        def _():
            weights(turn)

        @at(jnp.logical_and(hub, within(turn - 1)))
        def _():
            combine(turn - 1)

        @at(jnp.logical_and(rim, within(turn - 1)))
        def _():
            pass_on(turn - 1)

        @at(jnp.logical_and(rim, within(turn - 2)))
        def _():
            close(turn - 2)

        @at(within(s - out_begin))
        def _():
            output(s - out_begin)

        for o in range(nh):
            @at(s == by_z(TG) + (o - 1) % nh)
            def _():
                input_part(o)

        @at(s == out_begin + pairs)
        def _():
            strict_ones = (row_ids > col_ids).astype(f32)
            which = lax.broadcasted_iota(jnp.int32, (heads, pairs), 0) // per
            row = (which == lax.broadcasted_iota(jnp.int32, (heads, pairs), 1)).astype(f32)
            mine = (lax.rem(lax.broadcasted_iota(jnp.int32, (heads, LANES), 0), per)
                    == lax.broadcasted_iota(jnp.int32, (heads, LANES), 1) // hdim)
            through = jnp.sum(jnp.where(mine, dot_exact(row, th_s[...]), 0.0), axis=1, keepdims=True)
            dg_ref[...] = (dot_exact(q1_s[...], lower_ones, ROWS)
                           + dot_exact(q2_s[...], strict_ones, (((0,), (1,)), ((), ()))) + through)

        @at(s == total_slots - 3)
        def _():
            total = part[0]
            for o in range(1, nh):
                g_copy(o).wait()
                total = total + got[o]
            tg_ref[...] = jnp.transpose(total).astype(bf16)

        return carry

    total_slots = w_rest + pairs + 2 - (w_rest - w_first) // w_gap
    lax.fori_loop(0, total_slots, slot_step, 0)

    t_far().wait_send()

    @pl.when(hub)
    def _():
        for slot in range(3):
            for i in range(2):
                core_copy(slot, i).wait_send()
            if slot:
                x_copy(slot).wait_send()

    @pl.when(rim)
    def _():
        t_near(0, h).wait_send()
        t_near(1, hx).wait_send()

    def drain(k, carry):
        @pl.when(k < pairs // 2)
        def _():
            for kind in range(2):
                lane_copy(kind, k).wait_send()
                result_copy(kind, k, 2 * k + y).wait_send()

                @pl.when(z != (0, n // 2 - 1)[kind])
                def _():
                    next_copy(kind, k).wait_send()

        pg_copy(k).wait_send()

        @pl.when(hub)
        def _():
            relay_copy(k).wait_send()
            y_copy(k).wait_send()
            rim_copy(k).wait_send()
            a_copy(k).wait_send()
            b_copy(k).wait_send()

        @pl.when(rim)
        def _():
            o_copy(k).wait_send()

        return carry

    lax.fori_loop(0, pairs, drain, 0)


def hub_call(*args):
    n, nh = lax.axis_size("seq"), lax.axis_size("head")
    tokens, x_weight, b_input, _, log_decay, _, cotangent = args
    rows, width = cotangent.shape
    depth = tokens.shape[1]
    heads, state = log_decay.shape[0], b_input.shape[1]
    pairs = width // LANES
    half, unit, quarter, tcols = depth // 2, depth // (2 * n), rows // nh, depth // nh
    vm = pl.BlockSpec(memory_space=pltpu.VMEM)
    anywhere = pl.BlockSpec(memory_space=pl.ANY)
    dma = pltpu.SemaphoreType.DMA
    wide = pltpu.VMEM((pairs, rows, LANES), f32)

    def states(more=0, split=1):
        return pltpu.VMEM((pairs // split, state + more, LANES), f32)

    def blocks(count):
        return pltpu.VMEM((pairs, count * unit, LANES), f32)

    scratch = [
        pltpu.VMEM((pairs, rows, LANES), bf16), wide, wide, wide, pltpu.VMEM((heads, rows), f32),
        wide, wide, wide, pltpu.VMEM((rows, rows), f32), states(), states(8), states(0, 2), states(8, 2),
        states(0, 2), states(0, 2), states(0, 2), states(0, 2), states(0, 2), states(0, 2), states(), states(),
        pltpu.VMEM((rows, heads), f32), pltpu.VMEM((rows, heads), f32), pltpu.VMEM((pairs, LANES), f32),
        pltpu.VMEM(x_weight.shape, bf16), pltpu.VMEM(tokens.shape, bf16), pltpu.VMEM(cotangent.shape, bf16),
        wide, pltpu.VMEM((width, rows), bf16),
        pltpu.VMEM((3, pairs, rows, LANES), f32), pltpu.VMEM((3, quarter, half), f32),
        pltpu.VMEM((3, nh, quarter, half), f32), pltpu.VMEM((half, 4 * rows), bf16),
        blocks(3), blocks(3), blocks(2), blocks(1), blocks(3), blocks(1),
        pltpu.VMEM((nh, tcols, rows), f32), pltpu.VMEM((nh, tcols, rows), f32),
        dma((3,)), dma((2, 3, pairs // 2)), dma((2, 3, pairs // 2)),
        dma((pairs,)), dma((3, pairs)), dma((pairs,)), dma((3,)), dma((3, nh)), dma((3, 2)), dma((3,)),
        dma((2, pairs)), dma((2, pairs)), dma((pairs,)), dma((pairs,)), dma((pairs,)), dma((pairs,)),
        dma((pairs,)), dma((pairs,)), dma((nh,)), dma((nh,))]
    outs = [jax.ShapeDtypeStruct((rows, width), bf16), jax.ShapeDtypeStruct((heads, rows), f32),
            jax.ShapeDtypeStruct((depth // n, width), f32), jax.ShapeDtypeStruct((rows, tcols), bf16)]
    return pl.pallas_call(
        functools.partial(hub_kernel, n, nh),
        out_shape=outs,
        in_specs=[anywhere] * 2 + [vm] * 4 + [anywhere],
        out_specs=[vm] * len(outs),
        scratch_shapes=scratch,
        compiler_params=pltpu.CompilerParams(
            collective_id=1, has_side_effects=True, vmem_limit_bytes=60 << 20),
        cost_estimate=pl.CostEstimate(
            flops=6 * rows * depth * width, bytes_accessed=12 << 20, transcendentals=1 << 20),
        name="hub",
    )(*args)


def hand_kernel(count, *refs):
    ins, outs, mids = refs[:count], refs[count:2 * count], refs[2 * count:3 * count]
    sems = refs[3 * count]
    first = [pltpu.make_async_copy(a, m, sems.at[0, i]) for i, (a, m) in enumerate(zip(ins, mids))]
    second = [pltpu.make_async_copy(m, b, sems.at[1, i]) for i, (m, b) in enumerate(zip(mids, outs))]
    for copy in first:
        copy.start()
    for one, two in zip(first, second):
        one.wait()
        two.start()
    for copy in second:
        copy.wait()


def hand_over(*arrays):
    anywhere = pl.BlockSpec(memory_space=pl.ANY)
    count = len(arrays)
    return pl.pallas_call(
        functools.partial(hand_kernel, count),
        out_shape=[jax.ShapeDtypeStruct(a.shape, a.dtype) for a in arrays],
        in_specs=[anywhere] * count,
        out_specs=[anywhere] * count,
        scratch_shapes=[pltpu.VMEM(a.shape, a.dtype) for a in arrays]
        + [pltpu.SemaphoreType.DMA((2, count))],
        name="hand_over",
    )(*arrays)


def per_device(tokens, x_weight, b_input, c_input, log_decay, step_size, cotangent):
    n, nh = lax.axis_size("seq"), lax.axis_size("head")
    rows, depth = tokens.shape
    assert rows == SPAN and n % 2 == 0
    args = (tokens, x_weight, b_input, c_input, log_decay.T, step_size.T, cotangent)
    if n == 8 and nh == 4:
        y, dg, wg, tg = hub_call(*args)
        y, wg, tg = hand_over(y, wg, tg)
        return y, tg, wg, dg.T
    y, pg, dg = span_call(n, *args)
    pgb = pg.astype(bf16)
    wg = lax.psum_scatter(dot_f32(tokens, pgb, ROWS), "seq", scatter_dimension=0, tiled=True)
    tg = lax.psum_scatter(dot_f32(pgb, x_weight, COLS), "head", scatter_dimension=1, tiled=True)
    return y, tg.astype(bf16), wg, dg.T


def solution(mesh):
    return jax.shard_map(
        per_device,
        mesh=mesh,
        in_specs=(
            P("seq", None),
            P(None, "head"),
            P("seq", None),
            P("seq", None),
            P("seq", "head"),
            P("seq", "head"),
            P("seq", "head"),
        ),
        out_specs=(P("seq", "head"), P("seq", "head"), P("seq", "head"), P("seq", "head")),
        check_vma=False,
    )
```
